256 devices in a mesh: lat: 4 (over y_hi, core), lon: 64 (over y_lo, z, x).
Axes of the slice: x: 4, y: 4 (y_hi: 2, y_lo: 2; y = y_hi * 2 + y_lo), z: 8, core: 2. Of those that a mesh axis runs over, the one named last changes fastest.
Arguments:
- inputs: bfloat16 [8, 24, 768, 192], P(None, 'lat', 'lon'), may hold values from -6 to 6
- cotangent: bfloat16 [8, 24, 768, 192], P(None, 'lat', 'lon'), may hold values from -6 to 6
- qkv_weight: bfloat16 [192, 576], P(None, 'lon'), may hold values from -0.4375 to 0.4375
- proj_weight: bfloat16 [192, 192], P(None, 'lon'), may hold values from -0.4375 to 0.4375
- up_weight: bfloat16 [192, 768], P(None, 'lon'), may hold values from -0.4375 to 0.4375
- down_weight: bfloat16 [768, 192], P(None, 'lon'), may hold values from -0.21875 to 0.21875
- norm_gains: bfloat16 [2, 192], P(None, 'lon'), may hold values from 0.099609375 to 1.8984375
- bias_table: bfloat16 [16, 6, 20736], P(None, None, 'lon'), may hold values from -4 to 304
- type_of: int32 [4, 4], replicated, may hold values from 0 to 15
- region: int32 [8, 24], P(None, 'lat'), may hold values from 0 to 2
Outputs:
- grad_input: bfloat16 [8, 24, 768, 192], P(None, 'lat', 'lon')
- grad_qkv: float32 [192, 576], P(None, 'lon')
- grad_proj: float32 [192, 192], P(None, 'lon')
- grad_up: float32 [192, 768], P(None, 'lon')
- grad_down: float32 [768, 192], P(None, 'lon')
- grad_gains: float32 [2, 192], P(None, 'lon')
- grad_table: float32 [16, 6, 20736], P(None, None, 'lon')
The draws below stay inside these ranges and needn't reach their ends.
Inputs may be any that keep to these rules, and one draw needn't show every extreme that they name: `type_of`: types may repeat and some may be absent. Attention joins only tokens of a window with equal region ids.
All inputs are finite; a program needn't handle non-finite values.
Results may differ from the reference program's by a relative error of at most 0.015.
Values may be sent and summed in bfloat16 or wider, within the bound.
No kernel may reach another device: no remote copies, remote signals or barrier semaphores. Data moves between devices by JAX's collectives and lax.ppermute only.
A program may use at most 64 MiB of HBM per device.

```python
import math
import jax
import jax.numpy as jnp
from jax import lax

WPL = 2
WLAT = 6
WLON = 12
WIN = 144
D = 192
HEADS = 6
FFN = 768
PLW = 4
LATW_DEV = 1
PLEV = 8
LAT_ROWS = 24
LON_COLS = 768
TYPES = 16
TOKENS = 147456
N_LAT = 4


def draw_bias_table(key, part):
    key_base = jax.random.fold_in(key, 0)
    base_vals = jnp.clip(jax.random.normal(key_base, (TYPES, HEADS, WIN, WIN), jnp.float32), -4.0, 4.0)
    return base_vals.reshape(TYPES, HEADS, WIN * WIN).astype(jnp.bfloat16)


def with_ends(values, own_key, smallest, high):
    longest = values.shape.index(max(values.shape))
    spots = []
    for shift in (0, 1):
        where = [jax.random.randint(jax.random.fold_in(own_key, axis), (), 0, length) for axis, length in enumerate(values.shape)]
        where[longest] = (where[longest] + shift) % values.shape[longest]
        spots.append(tuple(where))
    return values.at[spots[0]].set(smallest).at[spots[1]].set(high)


def levels(stream_key, dims, shards, smallest, top_value):
    def one(position, blocks):
        draws = jax.random.uniform(jax.random.fold_in(jax.random.fold_in(stream_key, 6), position), (blocks,), jnp.float32, smallest / len(shards), top_value / len(shards))
        return jnp.repeat(jnp.exp(draws), dims[position] // blocks).reshape((-1,) + (1,) * (len(dims) - position - 1))

    level = one(*shards[0])
    for cut in shards[1:]:
        level = level * one(*cut)
    return level


def bell_draw(key, extent, width, bound, pieces=(), held_as=jnp.bfloat16):
    loudness = levels(key, extent, pieces, -0.22, 0.18) if pieces else 1.0
    entries = jax.random.normal(key, extent, jnp.float32) * width * loudness
    return jnp.minimum(jnp.maximum(entries, -bound), bound).astype(held_as)


def setup_inputs(seed: int = 0) -> dict:
    splits = jax.random.split(jax.random.key(seed), 11)
    return {
        "inputs": bell_draw(splits[0], (PLEV, LAT_ROWS, LON_COLS, D), 1.0, 6.0, ((1, 4), (2, 64))),
        "cotangent": bell_draw(splits[1], (PLEV, LAT_ROWS, LON_COLS, D), 1.0, 6.0, ((1, 4), (2, 64))),
        "qkv_weight": bell_draw(splits[2], (D, 3 * D), D ** -0.5, 0.4375, ((1, 64),)),
        "proj_weight": bell_draw(splits[3], (D, D), D ** -0.5, 0.4375, ((1, 64),)),
        "up_weight": bell_draw(splits[4], (D, FFN), D ** -0.5, 0.4375, ((1, 64),)),
        "down_weight": bell_draw(splits[5], (FFN, D), FFN ** -0.5, 0.21875, ((1, 64),)),
        "norm_gains": jnp.clip(1.0 + 0.18 * jax.random.normal(splits[6], (2, D), jnp.float32), 0.099609375, 1.8984375).astype(jnp.bfloat16),
        "bias_table": draw_bias_table(jax.random.fold_in(splits[10], 71), 0),
        "type_of": with_ends(jax.random.randint(splits[8], (PLW, LATW_DEV * N_LAT), 0, TYPES), jax.random.fold_in(splits[8], 1), 0, TYPES - 1).astype(jnp.int32),
        "region": with_ends(jax.random.randint(splits[9], (PLEV, LAT_ROWS), 0, 3), jax.random.fold_in(splits[9], 1), 0, 2).astype(jnp.int32),
    }


def layer_norm(values):
    row_mean = lax.optimization_barrier(jnp.mean(values, axis=-1, keepdims=True))
    centred = values - row_mean
    variance = lax.optimization_barrier(jnp.mean(centred * centred, axis=-1, keepdims=True))
    inv_std = lax.rsqrt(variance + 1e-05)
    return (centred * inv_std, inv_std)

def norm_back(d_normed, normed, inv_std):
    return inv_std * (d_normed - lax.optimization_barrier(jnp.mean(d_normed, axis=-1, keepdims=True)) - normed * lax.optimization_barrier(jnp.mean(d_normed * normed, axis=-1, keepdims=True)))

def gelu_pair(pre_act):
    cumul = 0.5 * (1.0 + lax.erf(pre_act * 0.7071067811865476))
    density = jnp.exp(-0.5 * pre_act * pre_act) * 0.3989422804014327
    return (pre_act * cumul, cumul + pre_act * density)

def to_windows(column, level_windows, row_windows):
    features = column.shape[-1]
    shaped = column.reshape(level_windows, WPL, row_windows, WLAT, WLON, features)
    return shaped.transpose(0, 2, 1, 3, 4, 5).reshape(level_windows * row_windows * WIN, features)

def from_windows(flat, level_windows, row_windows):
    features = flat.shape[-1]
    shaped = flat.reshape(level_windows, row_windows, WPL, WLAT, WLON, features)
    return shaped.transpose(0, 2, 1, 3, 4, 5).reshape(level_windows * WPL, row_windows * WLAT, WLON, features)

def region_mask(region_rows, level_windows, row_windows):
    labels = region_rows.reshape(level_windows, WPL, row_windows, WLAT).transpose(0, 2, 1, 3)
    labels = jnp.broadcast_to(labels[..., None], (level_windows, row_windows, WPL, WLAT, WLON))
    labels = labels.reshape(level_windows, row_windows, WIN)
    return labels[..., :, None] == labels[..., None, :]

def column_grads(column, cot_column, weights, bias_pos, same_region):
    qkv_full, proj_full, up_full, down_full, gains_full = weights
    f32 = jnp.float32
    bf16 = jnp.bfloat16
    level_windows = column.shape[0] // WPL
    row_windows = column.shape[1] // WLAT
    features = column.shape[-1]
    head_count = bias_pos.shape[2]
    head_size = features // head_count
    factor = 1.0 / math.sqrt(head_size)
    gain_one = gains_full[0].astype(f32)
    gain_two = gains_full[1].astype(f32)
    window_cells = to_windows(column, level_windows, row_windows).astype(f32)
    normed_one, inv_one = layer_norm(window_cells)
    scaled_one = (normed_one * gain_one).astype(bf16)
    packed = jnp.dot(scaled_one, qkv_full, preferred_element_type=f32).astype(bf16)
    packed = packed.reshape(level_windows, row_windows, WIN, 3, head_count, head_size)
    queries = packed[:, :, :, 0]
    key_rows = packed[:, :, :, 1]
    value_rows = packed[:, :, :, 2]
    scores = jnp.einsum('abthd,abshd->abhts', queries.astype(f32), key_rows.astype(f32)) * factor
    scores = scores + bias_pos.astype(f32)
    scores = jnp.where(same_region[:, :, None], scores, -jnp.inf)
    peak_score = lax.optimization_barrier(jnp.max(scores, axis=-1, keepdims=True))
    raised = jnp.exp(scores - peak_score)
    attn_probs = raised / lax.optimization_barrier(jnp.sum(raised, axis=-1, keepdims=True))
    probs_b = attn_probs.astype(bf16)
    attended = jnp.einsum('abhts,abshd->abthd', probs_b.astype(f32), value_rows.astype(f32))
    attended = attended.astype(bf16).reshape(-1, features)
    middle = window_cells + jnp.dot(attended, proj_full, preferred_element_type=f32)
    normed_two, inv_two = layer_norm(middle)
    scaled_two = (normed_two * gain_two).astype(bf16)
    pre_act = jnp.dot(scaled_two, up_full, preferred_element_type=f32)
    activated, gelu_slope = gelu_pair(pre_act)
    hidden_b = activated.astype(bf16)
    cot_rows = to_windows(cot_column, level_windows, row_windows)
    grad_down = jnp.dot(hidden_b.T, cot_rows, preferred_element_type=f32)
    d_hidden = (jnp.dot(cot_rows, down_full.T, preferred_element_type=f32) * gelu_slope).astype(bf16)
    grad_up = jnp.dot(scaled_two.T, d_hidden, preferred_element_type=f32)
    d_htwo = jnp.dot(d_hidden, up_full.T, preferred_element_type=f32)
    gain_grad_two = lax.optimization_barrier(jnp.sum(d_htwo * normed_two, axis=0))
    d_middle = cot_rows.astype(f32) + norm_back(d_htwo * gain_two, normed_two, inv_two)
    d_middle_b = d_middle.astype(bf16)
    grad_proj = jnp.dot(attended.T, d_middle_b, preferred_element_type=f32)
    d_att = jnp.dot(d_middle_b, proj_full.T, preferred_element_type=f32).astype(bf16)
    d_att = d_att.reshape(level_windows, row_windows, WIN, head_count, head_size)
    d_prob = jnp.einsum('abthd,abshd->abhts', d_att.astype(f32), value_rows.astype(f32))
    d_values = jnp.einsum('abhts,abthd->abshd', probs_b.astype(f32), d_att.astype(f32))
    d_score = attn_probs * (d_prob - lax.optimization_barrier(jnp.sum(attn_probs * d_prob, axis=-1, keepdims=True)))
    d_score_b = d_score.astype(bf16)
    d_queries = jnp.einsum('abhts,abshd->abthd', d_score_b.astype(f32), key_rows.astype(f32)) * factor
    d_keys = jnp.einsum('abhts,abthd->abshd', d_score_b.astype(f32), queries.astype(f32)) * factor
    d_packed = jnp.stack([d_queries, d_keys, d_values], axis=3).astype(bf16).reshape(-1, 3 * features)
    grad_qkv = jnp.dot(scaled_one.T, d_packed, preferred_element_type=f32)
    d_hone = jnp.dot(d_packed, qkv_full.T, preferred_element_type=f32)
    gain_grad_one = lax.optimization_barrier(jnp.sum(d_hone * normed_one, axis=0))
    d_cells = d_middle + norm_back(d_hone * gain_one, normed_one, inv_one)
    d_column = from_windows(d_cells.astype(bf16), level_windows, row_windows)
    param_grads = (grad_qkv, grad_proj, grad_up, grad_down, jnp.stack([gain_grad_one, gain_grad_two]))
    table_grad = d_score.reshape(level_windows * row_windows, head_count, WIN * WIN)
    return (d_column, param_grads, table_grad)

def reference(inputs, cotangent, qkv_weight, proj_weight, up_weight, down_weight, norm_gains, bias_table, type_of, region):
    shifts = (-(WPL // 2), -(WLAT // 2), -(WLON // 2))
    shifted = jnp.roll(inputs, shifts, (0, 1, 2))
    cot_shifted = jnp.roll(cotangent, shifts, (0, 1, 2))
    lat_windows = LATW_DEV * N_LAT
    lon_windows = LON_COLS // WLON
    features = inputs.shape[-1]
    head_count = bias_table.shape[1]
    bias_pos = bias_table[type_of].reshape(PLW, lat_windows, head_count, WIN, WIN)
    same_region = region_mask(region, PLW, lat_windows)
    columns = shifted.reshape(PLEV, LAT_ROWS, lon_windows, WLON, features).transpose(2, 0, 1, 3, 4)
    cot_columns = cot_shifted.reshape(PLEV, LAT_ROWS, lon_windows, WLON, features).transpose(2, 0, 1, 3, 4)
    weights = (qkv_weight, proj_weight, up_weight, down_weight, norm_gains)

    def advance(totals, column_pair):
        d_column, param_grads, table_grad = column_grads(column_pair[0], column_pair[1], weights, bias_pos, same_region)
        return (jax.tree.map(jnp.add, totals, (param_grads, table_grad)), d_column)
    initial = (tuple((jnp.zeros(member.shape, jnp.float32) for member in weights)), jnp.zeros((PLW * lat_windows, head_count, WIN * WIN), jnp.float32))
    totals, d_columns = lax.scan(advance, initial, (columns, cot_columns))
    d_shifted = d_columns.transpose(1, 2, 0, 3, 4).reshape(PLEV, LAT_ROWS, LON_COLS, features)
    grad_input = jnp.roll(d_shifted, (WPL // 2, WLAT // 2, WLON // 2), (0, 1, 2))
    factor = 1.0 / math.sqrt(TOKENS)
    param_grads, table_sum = totals
    onehot = (type_of.reshape(-1)[:, None] == jnp.arange(TYPES, dtype=jnp.int32)[None, :]).astype(jnp.float32)
    grad_table = jnp.dot(onehot.T, table_sum.reshape(PLW * lat_windows, -1), precision=lax.Precision.HIGHEST).reshape(TYPES, head_count, WIN * WIN)
    return (grad_input, param_grads[0] * factor, param_grads[1] * factor, param_grads[2] * factor, param_grads[3] * factor, param_grads[4] * factor, grad_table)
```

```python
import math

import jax
import jax.numpy as jnp
from jax import lax
from jax.sharding import Mesh, PartitionSpec as P

WPL = 2
WLAT = 6
WLON = 12
WIN = 144
D = 192
HEADS = 6
HEAD = 32
FFN = 768
LON = ("yl", "z", "x")
LAT = ("yh", "core")
F32 = jnp.float32
BF16 = jnp.bfloat16


def passed_along(block, axes, distance):
    size = math.prod(lax.axis_size(a) for a in axes)
    return lax.ppermute(block, axes, [((i - distance) % size, i) for i in range(size)])


def layer_norm(values):
    row_mean = jnp.mean(values, axis=-1, keepdims=True)
    centred = values - row_mean
    variance = jnp.mean(centred * centred, axis=-1, keepdims=True)
    inv_std = lax.rsqrt(variance + 1e-05)
    return (centred * inv_std, inv_std)


def norm_back(d_normed, normed, inv_std):
    return inv_std * (
        d_normed
        - jnp.mean(d_normed, axis=-1, keepdims=True)
        - normed * jnp.mean(d_normed * normed, axis=-1, keepdims=True)
    )


def gelu_pair(pre_act):
    cumul = 0.5 * (1.0 + lax.erf(pre_act * 0.7071067811865476))
    density = jnp.exp(-0.5 * pre_act * pre_act) * 0.3989422804014327
    return (pre_act * cumul, cumul + pre_act * density)


def window_grads(cells, weights, bias, labels):
    qkv_t, proj_t, up_t, down_t, gains = weights
    count = cells.shape[0]
    gain_one = gains[0].astype(F32)
    gain_two = gains[1].astype(F32)
    rows = cells.reshape(-1, 2 * D)
    window_cells = rows[:, :D].astype(F32)
    cot_rows = rows[:, D:]
    factor = 1.0 / math.sqrt(HEAD)
    normed_one, inv_one = layer_norm(window_cells)
    scaled_one = (normed_one * gain_one).astype(BF16)
    packed = jnp.dot(scaled_one, qkv_t.T, preferred_element_type=F32).astype(BF16)
    packed = packed.reshape(count, WIN, 3, HEADS, HEAD)
    queries, key_rows, value_rows = packed[:, :, 0], packed[:, :, 1], packed[:, :, 2]
    scores = jnp.einsum("wthd,wshd->whts", queries, key_rows, preferred_element_type=F32) * factor
    scores = scores + bias.astype(F32)[None]
    same = labels[:, None] == labels[None, :]
    scores = jnp.where(same, scores, -jnp.inf)
    raised = jnp.exp(scores - jnp.max(scores, axis=-1, keepdims=True))
    attn_probs = raised / jnp.sum(raised, axis=-1, keepdims=True)
    probs_b = attn_probs.astype(BF16)
    attended = jnp.einsum("whts,wshd->wthd", probs_b, value_rows, preferred_element_type=F32)
    attended = attended.astype(BF16).reshape(-1, D)
    middle = window_cells + jnp.dot(attended, proj_t.T, preferred_element_type=F32)
    normed_two, inv_two = layer_norm(middle)
    scaled_two = (normed_two * gain_two).astype(BF16)
    pre_act = jnp.dot(scaled_two, up_t.T, preferred_element_type=F32)
    activated, gelu_slope = gelu_pair(pre_act)
    hidden_b = activated.astype(BF16)
    g_down_t = jnp.dot(cot_rows.T, hidden_b, preferred_element_type=F32)
    d_hidden = (jnp.dot(cot_rows, down_t, preferred_element_type=F32) * gelu_slope).astype(BF16)
    g_up_t = jnp.dot(d_hidden.T, scaled_two, preferred_element_type=F32)
    d_htwo = jnp.dot(d_hidden, up_t, preferred_element_type=F32)
    g_gain_two = jnp.sum(d_htwo * normed_two, axis=0)
    d_middle = cot_rows.astype(F32) + norm_back(d_htwo * gain_two, normed_two, inv_two)
    d_middle_b = d_middle.astype(BF16)
    g_proj_t = jnp.dot(d_middle_b.T, attended, preferred_element_type=F32)
    d_att = jnp.dot(d_middle_b, proj_t, preferred_element_type=F32).astype(BF16)
    d_att = d_att.reshape(count, WIN, HEADS, HEAD)
    d_prob = jnp.einsum("wthd,wshd->whts", d_att, value_rows, preferred_element_type=F32)
    d_values = jnp.einsum("whts,wthd->wshd", probs_b, d_att, preferred_element_type=F32)
    d_score = attn_probs * (d_prob - jnp.sum(attn_probs * d_prob, axis=-1, keepdims=True))
    d_score_b = d_score.astype(BF16)
    d_queries = (
        jnp.einsum("whts,wshd->wthd", d_score_b, key_rows, preferred_element_type=F32) * factor
    )
    d_keys = jnp.einsum("whts,wthd->wshd", d_score_b, queries, preferred_element_type=F32) * factor
    d_packed = jnp.stack([d_queries, d_keys, d_values], axis=2).astype(BF16).reshape(-1, 3 * D)
    g_qkv_t = jnp.dot(d_packed.T, scaled_one, preferred_element_type=F32)
    d_hone = jnp.dot(d_packed, qkv_t, preferred_element_type=F32)
    g_gain_one = jnp.sum(d_hone * normed_one, axis=0)
    d_cells = d_middle + norm_back(d_hone * gain_one, normed_one, inv_one)
    d_cells = d_cells.astype(BF16).reshape(count, WIN, D)
    g_gains = jnp.stack([g_gain_one, g_gain_two])
    return d_cells, (g_qkv_t, g_proj_t, g_up_t, g_down_t, g_gains), jnp.sum(d_score, axis=0)


def shards(
    inputs,
    cotangent,
    qkv_weight,
    proj_weight,
    up_weight,
    down_weight,
    norm_gains,
    bias_table,
    type_of,
    region,
):
    lat_index = lax.axis_index(LAT)
    core = lax.axis_index("core")
    x_index = lax.axis_index("x")
    type_count = bias_table.shape[0]
    positions = type_of.shape[0]
    own = bias_table.shape[2]
    groups = lax.axis_size("yl") * lax.axis_size("z")
    members = lax.axis_size("x")
    lons = groups * members

    flat = jnp.concatenate(
        [
            up_weight.T.reshape(-1),
            down_weight.T.reshape(-1),
            qkv_weight.T.reshape(-1),
            proj_weight.T.reshape(-1),
        ]
    )
    half_size = flat.shape[0] // 2
    half = lax.dynamic_index_in_dim(flat.reshape(2, half_size // 128, 128), core, 0, False)
    types = lax.dynamic_slice(type_of, (jnp.int32(0), lat_index), (positions, 1))[:, 0]
    onehot = types[:, None] == jnp.arange(type_count, dtype=jnp.int32)[None, :]
    slabs = jnp.dot(
        onehot.astype(BF16), bias_table.reshape(type_count, -1), preferred_element_type=F32
    ).astype(BF16)
    slabs = slabs.reshape(positions, HEADS, own)
    slabs = lax.dynamic_update_slice(
        jnp.zeros((positions, HEADS, 3 * WIN), BF16), slabs, (0, 0, x_index * 36)
    ).reshape(positions, -1)
    slab_size = slabs.shape[1]
    gain_part = jnp.broadcast_to(norm_gains.reshape(1, 6), (positions, 6))
    fill = jnp.zeros((positions, 21 * 128 - slab_size - 6), BF16)
    slabs = jnp.concatenate([slabs, gain_part, fill], axis=1).reshape(positions, 21, 128)
    parcel = jnp.concatenate([jnp.broadcast_to(half[None], (positions, 27, 128)), slabs], axis=1)
    parcel = jnp.broadcast_to(parcel[None], (groups, members, 48, 128)).reshape(lons, 48, 128)
    landed = lax.all_to_all(parcel, LON, 0, 0)

    halves = lax.all_gather(landed[:, :27], "core", axis=0).reshape(2, lons, half_size)
    up_t = halves[0, :, :2304].reshape(FFN, D)
    down_t = jnp.concatenate([halves[0, :, 2304:], halves[1, :, :1152]], axis=1).reshape(D, FFN)
    qkv_t = halves[1, :, 1152:2880].reshape(3 * D, D)
    proj_t = halves[1, :, 2880:].reshape(D, D)
    tail = landed[:, 27:].reshape(lons, 21 * 128)
    gains = tail[:, slab_size : slab_size + 6].reshape(lons, 2, 3).transpose(1, 0, 2).reshape(2, D)
    strips = tail[:, :slab_size].reshape(groups, members, HEADS, 3, WIN)
    joined = [
        strips[:, 0, :, 0],
        strips[:, 0, :, 1],
        strips[:, 0, :, 2] + strips[:, 1, :, 0],
        strips[:, 1, :, 1],
        strips[:, 1, :, 2] + strips[:, 2, :, 0],
        strips[:, 2, :, 1],
        strips[:, 2, :, 2] + strips[:, 3, :, 0],
        strips[:, 3, :, 1],
        strips[:, 3, :, 2],
    ]
    bias = jnp.stack(joined, axis=2).transpose(1, 0, 2, 3).reshape(HEADS, WIN, WIN)

    cells = jnp.concatenate([inputs, cotangent], axis=-1)
    cells = jnp.roll(cells, -1, axis=0)
    arrived = passed_along(cells[:, :3], LAT, -1)
    cells = jnp.concatenate([cells[:, 3:], arrived], axis=1)
    cells = cells.reshape(positions, WPL, WLAT, WLON, 2 * D)
    cells = lax.all_to_all(cells, "x", 0, 0)
    halo = passed_along(cells[0, :, :, :6], ("yl", "z"), -1)
    cells = cells.transpose(1, 2, 0, 3, 4).reshape(WPL, WLAT, members * WLON, 2 * D)
    cells = jnp.concatenate([cells[:, :, 6:], halo], axis=2)
    cells = cells.reshape(WPL, WLAT, members, WLON, 2 * D).transpose(2, 0, 1, 3, 4)
    cells = cells.reshape(members, WIN, 2 * D)

    labels = lax.dynamic_slice(region, (x_index * WPL, jnp.int32(0)), (WPL, WLAT))
    labels = jnp.broadcast_to(labels[:, :, None], (WPL, WLAT, WLON)).reshape(WIN)

    d_cells, grads, table_sum = window_grads(
        cells, (qkv_t, proj_t, up_t, down_t, gains), bias, labels
    )
    g_qkv_t, g_proj_t, g_up_t, g_down_t, g_gains = grads

    back = d_cells.reshape(members, WPL, WLAT, WLON, D).transpose(1, 2, 0, 3, 4)
    back = back.reshape(WPL, WLAT, members * WLON, D)
    halo = passed_along(back[:, :, -6:], ("yl", "z"), 1)
    back = jnp.concatenate([halo, back[:, :, :-6]], axis=2)
    back = back.reshape(WPL, WLAT, members, WLON, D).transpose(2, 0, 1, 3, 4)
    back = lax.all_to_all(back, "x", 0, 0).reshape(2 * positions, WLAT, WLON, D)
    arrived = passed_along(back[:, 3:], LAT, 1)
    back = jnp.concatenate([arrived, back[:, :3]], axis=1)
    grad_input = jnp.roll(back, 1, axis=0)

    g_flat = jnp.concatenate(
        [
            g_up_t.reshape(lons, -1),
            g_down_t.reshape(lons, -1),
            g_qkv_t.reshape(lons, -1),
            g_proj_t.reshape(lons, -1),
        ],
        axis=1,
    ).reshape(lons, 2, half_size)
    kept = lax.dynamic_index_in_dim(g_flat, core, 1, False)
    given = lax.dynamic_index_in_dim(g_flat, 1 - core, 1, False)
    g_half = kept + passed_along(given.astype(BF16), ("core",), 1).astype(F32)
    g_half = g_half.astype(BF16).reshape(lons, 27, 128)
    strips = table_sum.astype(BF16).reshape(HEADS, groups, 9, WIN)
    strips = jnp.stack([strips[:, :, 2 * i : 2 * i + 3] for i in range(members)], axis=2)
    strips = strips.transpose(1, 2, 0, 3, 4).reshape(lons, slab_size)
    g_gain_part = g_gains.reshape(2, lons, 3).transpose(1, 0, 2).reshape(lons, 6).astype(BF16)
    fill = jnp.zeros((lons, 21 * 128 - slab_size - 6), BF16)
    strips = jnp.concatenate([strips, g_gain_part, fill], axis=1).reshape(lons, 21, 128)
    returned = lax.all_to_all(jnp.concatenate([g_half, strips], axis=1), LON, 0, 0)
    returned = returned.astype(F32)
    half_sum = jnp.sum(returned[:, :27], axis=0).reshape(-1)
    strip_sum = jnp.sum(returned[:, 27:].reshape(groups, members, 21 * 128), axis=0)
    table_part = lax.dynamic_slice(
        strip_sum[:, :slab_size].reshape(positions, HEADS, 3 * WIN),
        (jnp.int32(0), jnp.int32(0), x_index * 36),
        (positions, HEADS, own),
    )
    gain_sum = jnp.sum(strip_sum[:, slab_size : slab_size + 6], axis=0)
    note = jnp.concatenate([half_sum, table_part.reshape(-1), gain_sum])
    size = note.shape[0]
    note = jnp.pad(note.astype(BF16), (0, -size % 1024)).reshape(-1, 128)
    notes = lax.all_gather(note, LAT, axis=0).astype(F32).reshape(4, -1)
    whole = jnp.sum(notes[:, :half_size].reshape(2, 2, half_size), axis=0).reshape(-1)
    table_size = positions * HEADS * own
    terms = notes[:, half_size : half_size + table_size].reshape(4 * positions, -1)
    gain_total = jnp.sum(notes[:, half_size + table_size : size], axis=0).reshape(2, 3)
    all_types = type_of.T.reshape(-1)
    select = jnp.arange(type_count, dtype=jnp.int32)[:, None] == all_types[None, :]
    grad_table = jnp.dot(select.astype(F32), terms, precision=lax.Precision.HIGHEST)
    factor = 1.0 / math.sqrt(inputs.shape[0] * inputs.shape[1] * inputs.shape[2] * 4 * lons)
    whole = whole * factor
    grad_up = whole[:2304].reshape(12, D).T
    grad_down = whole[2304:4608].reshape(3, FFN).T
    grad_qkv = whole[4608:6336].reshape(9, D).T
    grad_proj = whole[6336:].reshape(3, D).T
    return (
        grad_input,
        grad_qkv,
        grad_proj,
        grad_up,
        grad_down,
        gain_total * factor,
        grad_table.reshape(type_count, HEADS, own),
    )


def solution(mesh):
    finer = Mesh(mesh.devices.reshape(2, 2, 2, 8, 4), ("yh", "core", "yl", "z", "x"))
    return jax.shard_map(
        shards,
        mesh=finer,
        in_specs=(
            P(None, LAT, LON, None),
            P(None, LAT, LON, None),
            P(None, LON),
            P(None, LON),
            P(None, LON),
            P(None, LON),
            P(None, LON),
            P(None, None, LON),
            P(),
            P(None, LAT),
        ),
        out_specs=(
            P(None, LAT, LON, None),
            P(None, LON),
            P(None, LON),
            P(None, LON),
            P(None, LON),
            P(None, LON),
            P(None, None, LON),
        ),
        check_vma=False,
    )
```

```python
import math

import jax
import jax.numpy as jnp
from jax import lax
from jax.sharding import Mesh, PartitionSpec as P

WPL = 2
WLAT = 6
WLON = 12
WIN = 144
D = 192
HEADS = 6
HEAD = 32
FFN = 768
LON = ("yl", "z", "x")
LAT = ("yh", "core")
F32 = jnp.float32
BF16 = jnp.bfloat16


def passed_along(block, axes, distance):
    size = math.prod(lax.axis_size(a) for a in axes)
    return lax.ppermute(block, axes, [((i - distance) % size, i) for i in range(size)])


def layer_norm(values):
    row_mean = jnp.mean(values, axis=-1, keepdims=True)
    centred = values - row_mean
    variance = jnp.mean(centred * centred, axis=-1, keepdims=True)
    inv_std = lax.rsqrt(variance + 1e-05)
    return (centred * inv_std, inv_std)


def norm_back(d_normed, normed, inv_std):
    return inv_std * (
        d_normed
        - jnp.mean(d_normed, axis=-1, keepdims=True)
        - normed * jnp.mean(d_normed * normed, axis=-1, keepdims=True)
    )


def gelu_pair(pre_act):
    cumul = 0.5 * (1.0 + lax.erf(pre_act * 0.7071067811865476))
    density = jnp.exp(-0.5 * pre_act * pre_act) * 0.3989422804014327
    return (pre_act * cumul, cumul + pre_act * density)


def attend(cells, qkv_t, gain, bias, labels):
    count = cells.shape[0]
    window_cells = cells.reshape(-1, 2 * D)[:, :D].astype(F32)
    factor = 1.0 / math.sqrt(HEAD)
    normed, inv = layer_norm(window_cells)
    scaled = (normed * gain).astype(BF16)
    packed = jnp.dot(scaled, qkv_t.T, preferred_element_type=F32).astype(BF16)
    packed = packed.reshape(count, WIN, 3, HEADS, HEAD)
    queries, key_rows, value_rows = packed[:, :, 0], packed[:, :, 1], packed[:, :, 2]
    scores = jnp.einsum("wthd,wshd->whts", queries, key_rows, preferred_element_type=F32) * factor
    scores = scores + bias.astype(F32)[None]
    same = labels[:, None] == labels[None, :]
    scores = jnp.where(same, scores, -jnp.inf)
    raised = jnp.exp(scores - jnp.max(scores, axis=-1, keepdims=True))
    probs = raised / jnp.sum(raised, axis=-1, keepdims=True)
    attended = jnp.einsum(
        "whts,wshd->wthd", probs.astype(BF16), value_rows, preferred_element_type=F32
    )
    return attended.astype(BF16).reshape(-1, D), (normed, inv, scaled, packed, probs)


def feed_forward(cells, attended, proj_t, up_t, down_t, gain):
    rows = cells.reshape(-1, 2 * D)
    cot_rows = rows[:, D:]
    middle = rows[:, :D].astype(F32) + jnp.dot(attended, proj_t.T, preferred_element_type=F32)
    normed, inv = layer_norm(middle)
    scaled = (normed * gain).astype(BF16)
    pre_act = jnp.dot(scaled, up_t.T, preferred_element_type=F32)
    activated, gelu_slope = gelu_pair(pre_act)
    hidden_b = activated.astype(BF16)
    g_down_t = jnp.dot(cot_rows.T, hidden_b, preferred_element_type=F32)
    d_hidden = (jnp.dot(cot_rows, down_t, preferred_element_type=F32) * gelu_slope).astype(BF16)
    g_up_t = jnp.dot(d_hidden.T, scaled, preferred_element_type=F32)
    d_htwo = jnp.dot(d_hidden, up_t, preferred_element_type=F32)
    g_gain = jnp.sum(d_htwo * normed, axis=0)
    d_middle = cot_rows.astype(F32) + norm_back(d_htwo * gain, normed, inv)
    d_middle_b = d_middle.astype(BF16)
    g_proj_t = jnp.dot(d_middle_b.T, attended, preferred_element_type=F32)
    d_att = jnp.dot(d_middle_b, proj_t, preferred_element_type=F32).astype(BF16)
    return d_middle, d_att, g_proj_t, g_up_t, g_down_t, g_gain


def attend_back(saved, d_att, d_middle, qkv_t, gain):
    normed, inv, scaled, packed, probs = saved
    count = packed.shape[0]
    factor = 1.0 / math.sqrt(HEAD)
    queries, key_rows, value_rows = packed[:, :, 0], packed[:, :, 1], packed[:, :, 2]
    d_att = d_att.reshape(count, WIN, HEADS, HEAD)
    d_prob = jnp.einsum("wthd,wshd->whts", d_att, value_rows, preferred_element_type=F32)
    d_values = jnp.einsum("whts,wthd->wshd", probs.astype(BF16), d_att, preferred_element_type=F32)
    d_score = probs * (d_prob - jnp.sum(probs * d_prob, axis=-1, keepdims=True))
    d_score_b = d_score.astype(BF16)
    d_queries = (
        jnp.einsum("whts,wshd->wthd", d_score_b, key_rows, preferred_element_type=F32) * factor
    )
    d_keys = jnp.einsum("whts,wthd->wshd", d_score_b, queries, preferred_element_type=F32) * factor
    d_packed = jnp.stack([d_queries, d_keys, d_values], axis=2).astype(BF16).reshape(-1, 3 * D)
    g_qkv_t = jnp.dot(d_packed.T, scaled, preferred_element_type=F32)
    d_hone = jnp.dot(d_packed, qkv_t, preferred_element_type=F32)
    g_gain = jnp.sum(d_hone * normed, axis=0)
    d_cells = d_middle + norm_back(d_hone * gain, normed, inv)
    return d_cells.astype(BF16).reshape(count, WIN, D), g_qkv_t, jnp.sum(d_score, axis=0), g_gain


def shards(
    inputs,
    cotangent,
    qkv_weight,
    proj_weight,
    up_weight,
    down_weight,
    norm_gains,
    bias_table,
    type_of,
    region,
):
    lat_index = lax.axis_index(LAT)
    core = lax.axis_index("core")
    x_index = lax.axis_index("x")
    type_count = bias_table.shape[0]
    positions = type_of.shape[0]
    own = bias_table.shape[2]
    groups = lax.axis_size("yl") * lax.axis_size("z")
    members = lax.axis_size("x")
    lons = groups * members

    cells = jnp.concatenate([inputs, cotangent], axis=-1)
    cells = jnp.roll(cells, -1, axis=0)

    flat = jnp.concatenate(
        [
            up_weight.T.reshape(-1),
            down_weight.T.reshape(-1),
            qkv_weight.T.reshape(-1),
            proj_weight.T.reshape(-1),
        ]
    )
    half_size = flat.shape[0] // 2
    half = lax.dynamic_index_in_dim(flat.reshape(2, half_size // 128, 128), core, 0, False)
    types = lax.dynamic_slice(type_of, (jnp.int32(0), lat_index), (positions, 1))[:, 0]
    onehot = types[:, None] == jnp.arange(type_count, dtype=jnp.int32)[None, :]
    slabs = jnp.dot(
        onehot.astype(BF16), bias_table.reshape(type_count, -1), preferred_element_type=F32
    ).astype(BF16)
    slabs = slabs.reshape(positions, HEADS, own)
    slabs = lax.dynamic_update_slice(
        jnp.zeros((positions, HEADS, 3 * WIN), BF16), slabs, (0, 0, x_index * 36)
    ).reshape(positions, -1)
    slab_size = slabs.shape[1]
    gain_part = jnp.broadcast_to(norm_gains.reshape(1, 6), (positions, 6))
    fill = jnp.zeros((positions, 21 * 128 - slab_size - 6), BF16)
    slabs = jnp.concatenate([slabs, gain_part, fill], axis=1).reshape(positions, 21, 128)
    parcel = jnp.concatenate([jnp.broadcast_to(half[None], (positions, 27, 128)), slabs], axis=1)
    parcel = jnp.broadcast_to(parcel[None], (groups, members, 48, 128)).reshape(lons, 48, 128)
    parcel, cells = lax.optimization_barrier((parcel, cells))
    arrived = passed_along(cells[:, :3], LAT, -1)
    landed = lax.all_to_all(parcel, LON, 0, 0)

    halves = lax.all_gather(landed[:, :27], "core", axis=0).reshape(2, lons, half_size)
    up_t = halves[0, :, :2304].reshape(FFN, D)
    down_t = jnp.concatenate([halves[0, :, 2304:], halves[1, :, :1152]], axis=1).reshape(D, FFN)
    qkv_t = halves[1, :, 1152:2880].reshape(3 * D, D)
    proj_t = halves[1, :, 2880:].reshape(D, D)
    tail = landed[:, 27:].reshape(lons, 21 * 128)
    gains = tail[:, slab_size : slab_size + 6].reshape(lons, 2, 3).transpose(1, 0, 2).reshape(2, D)
    strips = tail[:, :slab_size].reshape(groups, members, HEADS, 3, WIN)
    joined = [
        strips[:, 0, :, 0],
        strips[:, 0, :, 1],
        strips[:, 0, :, 2] + strips[:, 1, :, 0],
        strips[:, 1, :, 1],
        strips[:, 1, :, 2] + strips[:, 2, :, 0],
        strips[:, 2, :, 1],
        strips[:, 2, :, 2] + strips[:, 3, :, 0],
        strips[:, 3, :, 1],
        strips[:, 3, :, 2],
    ]
    bias = jnp.stack(joined, axis=2).transpose(1, 0, 2, 3).reshape(HEADS, WIN, WIN)

    cells = jnp.concatenate([cells[:, 3:], arrived], axis=1)
    cells = cells.reshape(positions, WPL * WLAT, WLON, 2 * D)
    cells = jnp.concatenate([cells, cells[: members - 1]], axis=0)
    cells = lax.dynamic_slice_in_dim(cells, x_index, members, 0)
    blocks = [cells[0]] + [passed_along(cells[k], ("x",), k) for k in range(1, members)]
    lefts = [block[:, :6] for block in blocks]
    is_first = [x_index == k for k in range(members)]
    rim = lefts[0]
    for k in range(1, members):
        rim = jnp.where(is_first[k], lefts[k], rim)
    rim = passed_along(rim, ("yl", "z"), -1)
    is_last = [(x_index - k) % members == members - 1 for k in range(members)]
    windows = [
        jnp.concatenate([blocks[k][:, 6:], jnp.where(is_last[k], rim, lefts[k - 1])], axis=1)
        for k in range(members)
    ]
    cells = jnp.stack(windows).reshape(members, WIN, 2 * D)

    labels = lax.dynamic_slice(region, (x_index * WPL, jnp.int32(0)), (WPL, WLAT))
    labels = jnp.broadcast_to(labels[:, :, None], (WPL, WLAT, WLON)).reshape(WIN)

    gain_one, gain_two = gains[0].astype(F32), gains[1].astype(F32)
    attended, saved = attend(cells, qkv_t, gain_one, bias, labels)
    d_middle, d_att, g_proj_t, g_up_t, g_down_t, g_gain_two = feed_forward(
        cells, attended, proj_t, up_t, down_t, gain_two
    )
    d_cells, g_qkv_t, table_sum, g_gain_one = attend_back(saved, d_att, d_middle, qkv_t, gain_one)
    g_gains = jnp.stack([g_gain_one, g_gain_two])

    g_flat = jnp.concatenate(
        [
            g_up_t.reshape(lons, -1),
            g_down_t.reshape(lons, -1),
            g_qkv_t.reshape(lons, -1),
            g_proj_t.reshape(lons, -1),
        ],
        axis=1,
    ).reshape(lons, 2, half_size)
    kept = lax.dynamic_index_in_dim(g_flat, core, 1, False)
    given = lax.dynamic_index_in_dim(g_flat, 1 - core, 1, False)
    g_half = kept + passed_along(given.astype(BF16), ("core",), 1).astype(F32)
    g_half = g_half.astype(BF16).reshape(lons, 27, 128)
    strips = table_sum.astype(BF16).reshape(HEADS, groups, 9, WIN)
    strips = jnp.stack([strips[:, :, 2 * i : 2 * i + 3] for i in range(members)], axis=2)
    strips = strips.transpose(1, 2, 0, 3, 4).reshape(lons, slab_size)
    g_gain_part = g_gains.reshape(2, lons, 3).transpose(1, 0, 2).reshape(lons, 6).astype(BF16)
    fill = jnp.zeros((lons, 21 * 128 - slab_size - 6), BF16)
    strips = jnp.concatenate([strips, g_gain_part, fill], axis=1).reshape(lons, 21, 128)
    parcel = jnp.concatenate([g_half, strips], axis=1)
    parcel, d_cells = lax.optimization_barrier((parcel, d_cells))
    returned = lax.all_to_all(parcel, LON, 0, 0)
    back = d_cells.reshape(members, WPL * WLAT, WLON, D)
    rim = back[0, :, 6:]
    for k in range(1, members):
        rim = jnp.where(is_last[k], back[k, :, 6:], rim)
    rim = passed_along(rim, ("yl", "z"), 1)
    blocks = [
        jnp.concatenate(
            [jnp.where(is_first[k], rim, back[(k + 1) % members, :, 6:]), back[k, :, :6]], axis=1
        )
        for k in range(members)
    ]
    blocks = [blocks[0]] + [passed_along(blocks[k], ("x",), -k) for k in range(1, members)]
    back = jnp.stack(blocks + blocks[: members - 1])
    back = lax.dynamic_slice_in_dim(back, (members - x_index) % members, members, 0)
    back = back.reshape(2 * positions, WLAT, WLON, D)
    arrived = passed_along(back[:, 3:], LAT, 1)
    back = jnp.concatenate([arrived, back[:, :3]], axis=1)
    grad_input = jnp.roll(back, 1, axis=0)

    returned = returned.astype(F32)
    half_sum = jnp.sum(returned[:, :27], axis=0).reshape(-1)
    strip_sum = jnp.sum(returned[:, 27:].reshape(groups, members, 21 * 128), axis=0)
    table_part = lax.dynamic_slice(
        strip_sum[:, :slab_size].reshape(positions, HEADS, 3 * WIN),
        (jnp.int32(0), jnp.int32(0), x_index * 36),
        (positions, HEADS, own),
    )
    gain_sum = jnp.sum(strip_sum[:, slab_size : slab_size + 6], axis=0)
    note = jnp.concatenate([half_sum, table_part.reshape(-1), gain_sum])
    size = note.shape[0]
    note = jnp.pad(note.astype(BF16), (0, -size % 1024)).reshape(-1, 128)
    notes = lax.all_gather(note, LAT, axis=0).astype(F32).reshape(4, -1)
    whole = jnp.sum(notes[:, :half_size].reshape(2, 2, half_size), axis=0).reshape(-1)
    table_size = positions * HEADS * own
    terms = notes[:, half_size : half_size + table_size].reshape(4 * positions, -1)
    gain_total = jnp.sum(notes[:, half_size + table_size : size], axis=0).reshape(2, 3)
    all_types = type_of.T.reshape(-1)
    select = jnp.arange(type_count, dtype=jnp.int32)[:, None] == all_types[None, :]
    grad_table = jnp.dot(select.astype(F32), terms, precision=lax.Precision.HIGHEST)
    factor = 1.0 / math.sqrt(inputs.shape[0] * inputs.shape[1] * inputs.shape[2] * 4 * lons)
    whole = whole * factor
    grad_up = whole[:2304].reshape(12, D).T
    grad_down = whole[2304:4608].reshape(3, FFN).T
    grad_qkv = whole[4608:6336].reshape(9, D).T
    grad_proj = whole[6336:].reshape(3, D).T
    return (
        grad_input,
        grad_qkv,
        grad_proj,
        grad_up,
        grad_down,
        gain_total * factor,
        grad_table.reshape(type_count, HEADS, own),
    )


def solution(mesh):
    finer = Mesh(mesh.devices.reshape(2, 2, 2, 8, 4), ("yh", "core", "yl", "z", "x"))
    return jax.shard_map(
        shards,
        mesh=finer,
        in_specs=(
            P(None, LAT, LON, None),
            P(None, LAT, LON, None),
            P(None, LON),
            P(None, LON),
            P(None, LON),
            P(None, LON),
            P(None, LON),
            P(None, None, LON),
            P(),
            P(None, LAT),
        ),
        out_specs=(
            P(None, LAT, LON, None),
            P(None, LON),
            P(None, LON),
            P(None, LON),
            P(None, LON),
            P(None, LON),
            P(None, None, LON),
        ),
        check_vma=False,
    )
```

```python
import math

import jax
import jax.numpy as jnp
from jax import lax
from jax.experimental import pallas as pl
from jax.experimental.pallas import tpu as pltpu
from jax.sharding import Mesh, PartitionSpec as P

WPL = 2
WLAT = 6
WLON = 12
WIN = 144
D = 192
HEADS = 6
HEAD = 32
FFN = 768
LON = ("yl", "z", "x")
LAT = ("yh", "core")
F32 = jnp.float32
BF16 = jnp.bfloat16


def passed_along(block, axes, distance):
    size = math.prod(lax.axis_size(a) for a in axes)
    return lax.ppermute(block, axes, [((i - distance) % size, i) for i in range(size)])


def layer_norm(values):
    row_mean = jnp.mean(values, axis=-1, keepdims=True)
    centred = values - row_mean
    variance = jnp.mean(centred * centred, axis=-1, keepdims=True)
    inv_std = lax.rsqrt(variance + 1e-05)
    return (centred * inv_std, inv_std)


def norm_back(d_normed, normed, inv_std):
    return inv_std * (
        d_normed
        - jnp.mean(d_normed, axis=-1, keepdims=True)
        - normed * jnp.mean(d_normed * normed, axis=-1, keepdims=True)
    )


def gelu_pair(pre_act):
    cumul = 0.5 * (1.0 + lax.erf(pre_act * 0.7071067811865476))
    density = jnp.exp(-0.5 * pre_act * pre_act) * 0.3989422804014327
    return (pre_act * cumul, cumul + pre_act * density)


def spread(a, b, contract):
    return lax.dot_general(a, b, ((contract[0], contract[1]), ((), ())), preferred_element_type=F32)


def nt(a, b):
    return spread(a, b, ((1,), (1,)))


def nn(a, b):
    return spread(a, b, ((1,), (0,)))


def tn(a, b):
    return spread(a, b, ((0,), (0,)))


def swap_quarters(rows):
    return jnp.concatenate([rows[:36], rows[72:108], rows[36:72], rows[108:]], axis=0)


def unpack_weights(halves_ref, qkv_ref, proj_ref, up_ref, down_ref):
    def stack(pieces):
        return jnp.concatenate(pieces, axis=0).astype(BF16)

    for g in range(4):
        v = [[halves_ref[c, 16 * g + i].astype(F32) for i in range(16)] for c in range(2)]
        for c in range(2):
            rows = slice(c * 384 + 96 * g, c * 384 + 96 * (g + 1))
            up_ref[rows, :128] = stack([p[:6] for p in v[c]])
            up_ref[rows, 128:] = stack([p[6:9, s : s + 64] for p in v[c] for s in (0, 64)])
            for t in range(3):
                cols = slice(c * 384 + 128 * t, c * 384 + 128 * (t + 1))
                down_ref[48 * g : 48 * (g + 1), cols] = stack(
                    [p[9 + 3 * t : 12 + 3 * t] for p in v[c]]
                )
        rows = slice(144 * g, 144 * (g + 1))
        pairs = list(zip(v[0], v[1]))
        qkv_ref[rows, :128] = stack([q for a, b in pairs for q in (a[18:24], b[18:21])])
        qkv_ref[rows, 128:] = stack(
            [q for a, b in pairs for q in (a[24:27, :64], a[24:27, 64:], b[24:27, :64])]
        )
        rows = slice(48 * g, 48 * (g + 1))
        proj_ref[rows, :128] = stack([b[21:24] for b in v[1]])
        proj_ref[rows, 128:] = stack([b[24:27, 64:] for b in v[1]])


def pack_grads(core, g_qkv, g_proj, g_up, g_down, kept_ref):
    def tails(ref, at, gap):
        return [ref[at : at + 3, 128:], ref[at + gap : at + gap + 3, 128:]]

    for e in range(64):
        for c in range(2):
            at = c * 384 + 6 * e
            ups = [g_up[at : at + 6, :128], jnp.concatenate(tails(g_up, at, 3), axis=1)]
            downs = [
                g_down[3 * e : 3 * e + 3, c * 384 + 128 * t : c * 384 + 128 * (t + 1)]
                for t in range(3)
            ]
            if c == 0:
                rest = [g_qkv[9 * e : 9 * e + 6, :128]]
                ends = tails(g_qkv, 9 * e, 3)
            else:
                rest = [g_qkv[9 * e + 6 : 9 * e + 9, :128], g_proj[3 * e : 3 * e + 3, :128]]
                ends = [g_qkv[9 * e + 6 : 9 * e + 9, 128:], g_proj[3 * e : 3 * e + 3, 128:]]
            rest.append(jnp.concatenate(ends, axis=1))
            piece = jnp.concatenate(ups + downs + rest, axis=0).astype(BF16)
            kept_ref[c if core is None else jnp.where(core == c, 0, 1), e] = piece


def block_kernel(
    last_ref,
    core_ref,
    b0,
    b1,
    b2,
    b3,
    rim_ref,
    halves_ref,
    gains_ref,
    strips_ref,
    row_label_ref,
    col_label_ref,
    back_ref,
    back_rim_ref,
    packed_ref,
    g_gains_ref,
    table_ref,
    qkv_ref,
    proj_ref,
    up_ref,
    down_ref,
    g_qkv,
    g_proj,
    g_up,
    g_down,
    tokens,
    bias_full,
    probs,
    table_sum,
    s_one,
    s_two,
    att_all,
    hid_all,
    dhid_all,
    dmid_all,
    dpack_all,
    d_tokens,
    gain_sums,
):
    factor = 1.0 / math.sqrt(HEAD)
    last = last_ref[0]
    blocks = (b0, b1, b2, b3)
    place = lax.broadcasted_iota(jnp.int32, (WIN, 1), 0) % WLON
    is_left = place < WLON // 2
    same = row_label_ref[...] == col_label_ref[...]
    unpack_weights(halves_ref, qkv_ref, proj_ref, up_ref, down_ref)
    source = lax.broadcasted_iota(jnp.int32, (WIN, 192), 1)
    target = lax.broadcasted_iota(jnp.int32, (WIN, 192), 0)
    held = 9 * (source // 12) + 2 * (source // 3 % 4) + source % 3
    joins = (held == target).astype(F32).astype(BF16)
    for h in range(HEADS):
        bias_full[h] = jnp.where(same, nn(joins, strips_ref[h]), -jnp.inf)
        table_sum[h] = jnp.zeros((WIN, WIN), F32)
    gain_sums[...] = jnp.zeros_like(gain_sums)
    rim = swap_quarters(rim_ref[...].astype(F32))
    natural = [swap_quarters(b[...].astype(F32)) for b in blocks]
    for k in range(4):
        ahead = jnp.where(last == k, rim, natural[k - 1])
        fore = jnp.concatenate([natural[k][6:], natural[k][:6]], axis=0)
        rear = jnp.concatenate([ahead[-6:], ahead[:-6]], axis=0)
        tokens[k] = jnp.where(is_left, fore, rear)
    gain_one = gains_ref[0:1, :].astype(F32)
    gain_two = gains_ref[1:2, :].astype(F32)
    lane = lax.broadcasted_iota(jnp.int32, (1, D), 1) // HEAD
    masks = [(lane == h).astype(BF16) for h in range(HEADS)]

    def one_window(w, carry):
        at = pl.multiple_of(w * WIN, 16)
        rows = pl.ds(at, WIN)
        both = tokens[w]
        cells = both[:, :D]
        cot = both[:, D:]
        cot_b = cot.astype(BF16)
        normed_one, inv_one = layer_norm(cells)
        scaled_one = (normed_one * gain_one).astype(BF16)
        s_one[rows, :] = scaled_one
        queries = nt(scaled_one, qkv_ref[0:D, :]).astype(BF16)
        key_rows = nt(scaled_one, qkv_ref[D : 2 * D, :]).astype(BF16)
        values = nt(scaled_one, qkv_ref[2 * D :, :]).astype(BF16)
        attended = jnp.zeros((WIN, D), F32)
        for h in range(HEADS):
            scores = nt(queries * masks[h], key_rows) * factor + bias_full[h]
            raised = jnp.exp(scores - jnp.max(scores, axis=-1, keepdims=True))
            p = raised * (1.0 / jnp.sum(raised, axis=-1, keepdims=True))
            probs[h] = p
            attended = attended + nn(p.astype(BF16), values * masks[h])
        attended = attended.astype(BF16)
        att_all[rows, :] = attended
        middle = cells + nt(attended, proj_ref[...])
        normed_two, inv_two = layer_norm(middle)
        scaled_two = (normed_two * gain_two).astype(BF16)
        s_two[rows, :] = scaled_two
        d_htwo = jnp.zeros((WIN, D), F32)
        for c in range(3):
            part = slice(c * 256, (c + 1) * 256)
            pre_act = nt(scaled_two, up_ref[part, :])
            activated, slope = gelu_pair(pre_act)
            hid_all[rows, part] = activated.astype(BF16)
            d_hidden = (nn(cot_b, down_ref[:, part]) * slope).astype(BF16)
            dhid_all[rows, part] = d_hidden
            d_htwo = d_htwo + nn(d_hidden, up_ref[part, :])
        gain_sums[1:2, :] += jnp.sum(d_htwo * normed_two, axis=0, keepdims=True)
        d_middle = cot + norm_back(d_htwo * gain_two, normed_two, inv_two)
        d_middle_b = d_middle.astype(BF16)
        dmid_all[rows, :] = d_middle_b
        d_att = nn(d_middle_b, proj_ref[...]).astype(BF16)
        d_queries = jnp.zeros((WIN, D), F32)
        d_keys = jnp.zeros((WIN, D), F32)
        d_values = jnp.zeros((WIN, D), F32)
        for h in range(HEADS):
            p = probs[h]
            d_att_h = d_att * masks[h]
            d_prob = nt(d_att_h, values)
            d_values = d_values + tn(p.astype(BF16), d_att_h)
            d_score = p * (d_prob - jnp.sum(p * d_prob, axis=-1, keepdims=True))
            table_sum[h] += d_score
            d_score_b = d_score.astype(BF16)
            d_queries = d_queries + nn(d_score_b, key_rows * masks[h])
            d_keys = d_keys + tn(d_score_b, queries * masks[h])
        d_q = (d_queries * factor).astype(BF16)
        d_k = (d_keys * factor).astype(BF16)
        d_v = d_values.astype(BF16)
        dpack_all[0, rows, :] = d_q
        dpack_all[1, rows, :] = d_k
        dpack_all[2, rows, :] = d_v
        d_hone = (
            nn(d_q, qkv_ref[0:D, :]) + nn(d_k, qkv_ref[D : 2 * D, :]) + nn(d_v, qkv_ref[2 * D :, :])
        )
        gain_sums[0:1, :] += jnp.sum(d_hone * normed_one, axis=0, keepdims=True)
        d_tokens[w] = d_middle + norm_back(d_hone * gain_one, normed_one, inv_one)
        return carry

    lax.fori_loop(0, 4, one_window, 0)
    for k in range(4):
        mine, following = d_tokens[k], d_tokens[(k + 1) % 4]
        fore = jnp.concatenate([mine[-6:], mine[:-6]], axis=0)
        rear = jnp.concatenate([following[6:], following[:6]], axis=0)
        first = (k + 1) % 4 == last
        back_ref[k] = swap_quarters(
            jnp.where(is_left, jnp.where(first, 0.0, rear), fore)
        ).astype(BF16)

        @pl.when(first)
        def _():
            back_rim_ref[...] = swap_quarters(jnp.where(is_left, rear, 0.0)).astype(BF16)

    for part in range(3):
        g_qkv[part * D : (part + 1) * D, :] = tn(dpack_all[part], s_one[...])
    g_proj[...] = tn(dmid_all[...], att_all[...])
    cots = jnp.concatenate([tokens[k][:, D:] for k in range(4)], axis=0).astype(BF16)
    g_down[...] = tn(cots, hid_all[...])
    g_up[...] = tn(dhid_all[...], s_two[...])
    g_gains_ref[...] = gain_sums[...]
    pack_grads(core_ref[0], g_qkv, g_proj, g_up, g_down, packed_ref)
    for h in range(HEADS):
        table_ref[h] = tn(joins, table_sum[h].astype(BF16)).astype(BF16)


def block_grads(last, core, blocks, rim, halves, gains, strips, row_label, col_label):
    rows = 4 * WIN
    out = [
        ((4, WIN, D), BF16),
        ((WIN, D), BF16),
        ((2, 64, 27, 128), BF16),
        ((2, D), F32),
        ((HEADS, 192, WIN), BF16),
    ]
    scratch = [
        ((3 * D, D), BF16),
        ((D, D), BF16),
        ((FFN, D), BF16),
        ((D, FFN), BF16),
        ((3 * D, D), F32),
        ((D, D), F32),
        ((FFN, D), F32),
        ((D, FFN), F32),
        ((4, WIN, 2 * D), F32),
        ((HEADS, WIN, WIN), F32),
        ((HEADS, WIN, WIN), F32),
        ((HEADS, WIN, WIN), F32),
        ((rows, D), BF16),
        ((rows, D), BF16),
        ((rows, D), BF16),
        ((rows, FFN), BF16),
        ((rows, FFN), BF16),
        ((rows, D), BF16),
        ((3, rows, D), BF16),
        ((4, WIN, D), F32),
        ((2, D), F32),
    ]
    whole = pl.BlockSpec(memory_space=pltpu.VMEM)
    return pl.pallas_call(
        block_kernel,
        in_specs=[pl.BlockSpec(memory_space=pltpu.SMEM)] * 2 + [whole] * 10,
        out_specs=[whole] * len(out),
        out_shape=[jax.ShapeDtypeStruct(s, t) for s, t in out],
        scratch_shapes=[pltpu.VMEM(s, t) for s, t in scratch],
        compiler_params=pltpu.CompilerParams(vmem_limit_bytes=48 << 20),
        name="block_grads",
    )(last.reshape(1), core.reshape(1), *blocks, rim, halves, gains, strips, row_label, col_label)


def shards(
    inputs,
    cotangent,
    qkv_weight,
    proj_weight,
    up_weight,
    down_weight,
    norm_gains,
    bias_table,
    type_of,
    region,
):
    lat_index = lax.axis_index(LAT)
    core = lax.axis_index("core")
    x_index = lax.axis_index("x")
    type_count = bias_table.shape[0]
    positions = type_of.shape[0]
    own = bias_table.shape[2]
    groups = lax.axis_size("yl") * lax.axis_size("z")
    members = lax.axis_size("x")
    lons = groups * members

    cells = jnp.concatenate([inputs, cotangent], axis=-1)
    cells = jnp.roll(cells, -1, axis=0).reshape(positions, WPL, 2, WLAT // 2, WLON, 2 * D)
    cells = cells.transpose(0, 2, 1, 3, 4, 5).reshape(positions, 2, WIN // 2, 2 * D)

    rows = jnp.concatenate([qkv_weight.T, proj_weight.T], axis=0)
    rows = jnp.stack([up_weight.T.reshape(2, 6, D), rows.reshape(2, 6, D)], axis=1)
    ends = rows[..., 128:].reshape(2, 2, 2, 3, 64).transpose(0, 1, 3, 2, 4).reshape(2, 2, 3, 128)
    downs = down_weight.reshape(lons, 2, 6, 3).transpose(1, 3, 0, 2).reshape(2, 3, 3, 128)
    downs = downs.transpose(0, 2, 1, 3).reshape(2, 9, 128)
    both = jnp.concatenate([rows[..., :128], ends], axis=2)
    half = jnp.concatenate([both[:, 0], downs, both[:, 1]], axis=1)
    half = lax.dynamic_index_in_dim(half, core, 0, False)
    types = lax.dynamic_slice(type_of, (jnp.int32(0), lat_index), (positions, 1))[:, 0]
    onehot = types[:, None] == jnp.arange(type_count, dtype=jnp.int32)[None, :]
    slabs = jnp.dot(
        onehot.astype(BF16), bias_table.reshape(type_count, -1), preferred_element_type=F32
    ).astype(BF16)
    slabs = slabs.reshape(positions, HEADS, own)
    slabs = lax.dynamic_update_slice(
        jnp.zeros((positions, HEADS, 3 * WIN), BF16), slabs, (0, 0, x_index * 36)
    ).reshape(positions, -1)
    slab_size = slabs.shape[1]
    gain_part = jnp.broadcast_to(norm_gains.reshape(1, 6), (positions, 6))
    fill = jnp.zeros((positions, 21 * 128 - slab_size - 6), BF16)
    slabs = jnp.concatenate([slabs, gain_part, fill], axis=1).reshape(positions, 21, 128)
    parcel = jnp.concatenate([jnp.broadcast_to(half[None], (positions, 27, 128)), slabs], axis=1)
    parcel = jnp.broadcast_to(parcel[None], (groups, members, 48, 128)).reshape(lons, 48, 128)
    parcel, cells = lax.optimization_barrier((parcel, cells))
    arrived = passed_along(cells[:, 0], LAT, -1)
    landed = lax.all_to_all(parcel, LON, 0, 0)

    halves = lax.all_gather(landed[:, :27], "core", axis=0)
    tail = landed[:, 27:].reshape(lons, 21 * 128)
    gains = tail[:, slab_size : slab_size + 6].reshape(lons, 2, 3).transpose(1, 0, 2).reshape(2, D)
    strips = tail[:, :slab_size].reshape(lons, HEADS, 3, WIN).transpose(1, 0, 2, 3)
    strips = strips.reshape(HEADS, 3 * lons, WIN)

    cells = jnp.concatenate([cells[:, 1], arrived], axis=1)
    cells = jnp.concatenate([cells, cells[: members - 1]], axis=0)
    cells = lax.dynamic_slice_in_dim(cells, x_index, members, 0)
    blocks = [cells[0]] + [passed_along(cells[k], ("x",), k) for k in range(1, members)]
    is_first = [x_index == k for k in range(members)]
    rim = blocks[0]
    for k in range(1, members):
        rim = jnp.where(is_first[k], blocks[k], rim)
    rim = passed_along(rim, ("yl", "z"), -1)
    last = (x_index + 1) % members

    labels = lax.dynamic_slice(region, (x_index * WPL, jnp.int32(0)), (WPL, WLAT))
    labels = jnp.broadcast_to(labels[:, :, None], (WPL, WLAT, WLON)).reshape(WIN)
    back, rim, packed, g_gains, strips = block_grads(
        last, core, blocks, rim, halves, gains, strips, labels.reshape(WIN, 1), labels.reshape(1, WIN)
    )

    g_half = packed[0].astype(F32) + passed_along(packed[1], ("core",), 1).astype(F32)
    g_half = g_half.astype(BF16)
    strips = strips.reshape(HEADS, lons, 3, WIN).transpose(1, 0, 2, 3).reshape(lons, slab_size)
    g_gain_part = g_gains.reshape(2, lons, 3).transpose(1, 0, 2).reshape(lons, 6).astype(BF16)
    fill = jnp.zeros((lons, 21 * 128 - slab_size - 6), BF16)
    strips = jnp.concatenate([strips, g_gain_part, fill], axis=1).reshape(lons, 21, 128)
    parcel = jnp.concatenate([g_half, strips], axis=1)
    parcel, rim = lax.optimization_barrier((parcel, rim))
    returned = lax.all_to_all(parcel, LON, 0, 0)
    rim = passed_along(rim, ("yl", "z"), 1)
    blocks = [jnp.where(is_first[k], back[k] + rim, back[k]) for k in range(members)]
    blocks = [blocks[0]] + [passed_along(blocks[k], ("x",), -k) for k in range(1, members)]
    back = jnp.stack(blocks + blocks[: members - 1])
    back = lax.dynamic_slice_in_dim(back, (members - x_index) % members, members, 0)
    back = back.reshape(positions, 2, WIN // 2, D)
    arrived = passed_along(back[:, 1], LAT, 1)
    back = jnp.stack([arrived, back[:, 0]], axis=1)
    back = back.reshape(positions, 2, WPL, WLAT // 2, WLON, D).transpose(0, 2, 1, 3, 4, 5)
    grad_input = jnp.roll(back.reshape(inputs.shape), 1, axis=0)

    returned = returned.astype(F32)
    half_sum = jnp.sum(returned[:, :27], axis=0).reshape(-1)
    half_size = half_sum.shape[0]
    strip_sum = jnp.sum(returned[:, 27:].reshape(groups, members, 21 * 128), axis=0)
    table_part = lax.dynamic_slice(
        strip_sum[:, :slab_size].reshape(positions, HEADS, 3 * WIN),
        (jnp.int32(0), jnp.int32(0), x_index * 36),
        (positions, HEADS, own),
    )
    gain_sum = jnp.sum(strip_sum[:, slab_size : slab_size + 6], axis=0)
    note = jnp.concatenate([half_sum, table_part.reshape(-1), gain_sum])
    size = note.shape[0]
    note = jnp.pad(note.astype(BF16), (0, -size % 1024)).reshape(-1, 128)
    notes = lax.all_gather(note, LAT, axis=0).astype(F32).reshape(4, -1)
    whole = jnp.sum(notes[:, :half_size].reshape(2, 2, 27, 128), axis=0)
    table_size = positions * HEADS * own
    terms = notes[:, half_size : half_size + table_size].reshape(4 * positions, -1)
    gain_total = jnp.sum(notes[:, half_size + table_size : size], axis=0).reshape(2, 3)
    all_types = type_of.T.reshape(-1)
    select = jnp.arange(type_count, dtype=jnp.int32)[:, None] == all_types[None, :]
    grad_table = jnp.dot(select.astype(F32), terms, precision=lax.Precision.HIGHEST)
    factor = 1.0 / math.sqrt(inputs.shape[0] * inputs.shape[1] * inputs.shape[2] * 4 * lons)
    whole = whole * factor

    def joined(at):
        ends = whole[:, at + 6 : at + 9].reshape(2, 3, 2, 64).transpose(0, 2, 1, 3)
        rows = jnp.concatenate([whole[:, at : at + 6], ends.reshape(2, 6, 64)], axis=2)
        return rows.reshape(12, D)

    grad_up = joined(0).T
    rows = joined(18)
    grad_qkv = rows[:9].T
    grad_proj = rows[9:].T
    grad_down = whole[:, 9:18].reshape(2, 3, 3, 128).transpose(0, 2, 1, 3).reshape(2, 3, lons, 6)
    grad_down = grad_down.transpose(2, 0, 3, 1).reshape(FFN, 3)
    return (
        grad_input,
        grad_qkv,
        grad_proj,
        grad_up,
        grad_down,
        gain_total * factor,
        grad_table.reshape(type_count, HEADS, own),
    )


def solution(mesh):
    finer = Mesh(mesh.devices.reshape(2, 2, 2, 8, 4), ("yh", "core", "yl", "z", "x"))
    return jax.shard_map(
        shards,
        mesh=finer,
        in_specs=(
            P(None, LAT, LON, None),
            P(None, LAT, LON, None),
            P(None, LON),
            P(None, LON),
            P(None, LON),
            P(None, LON),
            P(None, LON),
            P(None, None, LON),
            P(),
            P(None, LAT),
        ),
        out_specs=(
            P(None, LAT, LON, None),
            P(None, LON),
            P(None, LON),
            P(None, LON),
            P(None, LON),
            P(None, LON),
            P(None, None, LON),
        ),
        check_vma=False,
    )
```

```python
import math

import jax
import jax.numpy as jnp
from jax import lax
from jax.experimental import pallas as pl
from jax.experimental.pallas import tpu as pltpu
from jax.sharding import Mesh, PartitionSpec as P

WPL = 2
WLAT = 6
WLON = 12
WIN = 144
D = 192
HEADS = 6
HEAD = 32
FFN = 768
LON = ("yl", "z", "x")
LAT = ("yh", "core")
F32 = jnp.float32
BF16 = jnp.bfloat16


def passed_along(block, axes, distance):
    size = math.prod(lax.axis_size(a) for a in axes)
    return lax.ppermute(block, axes, [((i - distance) % size, i) for i in range(size)])


def layer_norm(values):
    row_mean = jnp.mean(values, axis=-1, keepdims=True)
    centred = values - row_mean
    variance = jnp.mean(centred * centred, axis=-1, keepdims=True)
    inv_std = lax.rsqrt(variance + 1e-05)
    return (centred * inv_std, inv_std)


def norm_back(d_normed, normed, inv_std):
    return inv_std * (
        d_normed
        - jnp.mean(d_normed, axis=-1, keepdims=True)
        - normed * jnp.mean(d_normed * normed, axis=-1, keepdims=True)
    )


def gelu_pair(pre_act):
    cumul = 0.5 * (1.0 + lax.erf(pre_act * 0.7071067811865476))
    density = jnp.exp(-0.5 * pre_act * pre_act) * 0.3989422804014327
    return (pre_act * cumul, cumul + pre_act * density)


def spread(a, b, contract):
    return lax.dot_general(a, b, ((contract[0], contract[1]), ((), ())), preferred_element_type=F32)


def nt(a, b):
    return spread(a, b, ((1,), (1,)))


def nn(a, b):
    return spread(a, b, ((1,), (0,)))


def tn(a, b):
    return spread(a, b, ((0,), (0,)))


def swap_quarters(rows):
    return jnp.concatenate([rows[:36], rows[72:108], rows[36:72], rows[108:]], axis=0)


def unpack_weights(halves_ref, qkv_ref, proj_ref, up_ref, down_ref):
    def stack(pieces):
        return jnp.concatenate(pieces, axis=0).astype(BF16)

    for g in range(4):
        v = [[halves_ref[c, 16 * g + i].astype(F32) for i in range(16)] for c in range(2)]
        for c in range(2):
            rows = slice(c * 384 + 96 * g, c * 384 + 96 * (g + 1))
            up_ref[rows, :128] = stack([p[:6] for p in v[c]])
            up_ref[rows, 128:] = stack([p[6:9, s : s + 64] for p in v[c] for s in (0, 64)])
            for t in range(3):
                cols = slice(c * 384 + 128 * t, c * 384 + 128 * (t + 1))
                down_ref[48 * g : 48 * (g + 1), cols] = stack(
                    [p[9 + 3 * t : 12 + 3 * t] for p in v[c]]
                )
        rows = slice(144 * g, 144 * (g + 1))
        pairs = list(zip(v[0], v[1]))
        qkv_ref[rows, :128] = stack([q for a, b in pairs for q in (a[18:24], b[18:21])])
        qkv_ref[rows, 128:] = stack(
            [q for a, b in pairs for q in (a[24:27, :64], a[24:27, 64:], b[24:27, :64])]
        )
        rows = slice(48 * g, 48 * (g + 1))
        proj_ref[rows, :128] = stack([b[21:24] for b in v[1]])
        proj_ref[rows, 128:] = stack([b[24:27, 64:] for b in v[1]])


def pack_grads(core, g_qkv, g_proj, g_up, g_down, kept_ref, given_ref):
    def tails(ref, at, gap):
        return [ref[at : at + 3, 128:], ref[at + gap : at + gap + 3, 128:]]

    for e in range(64):
        pieces = []
        for c in range(2):
            at = c * 384 + 6 * e
            ups = [g_up[at : at + 6, :128], jnp.concatenate(tails(g_up, at, 3), axis=1)]
            downs = [
                g_down[3 * e : 3 * e + 3, c * 384 + 128 * t : c * 384 + 128 * (t + 1)]
                for t in range(3)
            ]
            if c == 0:
                rest = [g_qkv[9 * e : 9 * e + 6, :128]]
                ends = tails(g_qkv, 9 * e, 3)
            else:
                rest = [g_qkv[9 * e + 6 : 9 * e + 9, :128], g_proj[3 * e : 3 * e + 3, :128]]
                ends = [g_qkv[9 * e + 6 : 9 * e + 9, 128:], g_proj[3 * e : 3 * e + 3, 128:]]
            rest.append(jnp.concatenate(ends, axis=1))
            pieces.append(jnp.concatenate(ups + downs + rest, axis=0))
        kept_ref[e] = jnp.where(core == 0, pieces[0], pieces[1]).astype(BF16)
        given_ref[e] = jnp.where(core == 0, pieces[1], pieces[0]).astype(BF16)


def block_kernel(
    last_ref,
    core_ref,
    b0,
    b1,
    b2,
    b3,
    rim_ref,
    halves_ref,
    landed_ref,
    row_label_ref,
    col_label_ref,
    back_ref,
    back_rim_ref,
    kept_ref,
    given_ref,
    strips_ref,
    qkv_ref,
    proj_ref,
    up_ref,
    down_ref,
    g_qkv,
    g_proj,
    g_up,
    g_down,
    tokens,
    bias_full,
    probs,
    d_probs,
    probs_b,
    scores_b,
    heads_q,
    heads_d,
    table_sum,
    s_one,
    s_two,
    att_all,
    hid_all,
    dhid_all,
    dmid_all,
    dpack_all,
    d_tokens,
    gain_sums,
):
    factor = 1.0 / math.sqrt(HEAD)
    last = last_ref[0]
    blocks = (b0, b1, b2, b3)
    place = lax.broadcasted_iota(jnp.int32, (WIN, 1), 0) % WLON
    is_left = place < WLON // 2
    same = row_label_ref[...] == col_label_ref[...]
    unpack_weights(halves_ref, qkv_ref, proj_ref, up_ref, down_ref)
    source = lax.broadcasted_iota(jnp.int32, (WIN, 192), 1)
    target = lax.broadcasted_iota(jnp.int32, (WIN, 192), 0)
    held = 9 * (source // 12) + 2 * (source // 3 % 4) + source % 3
    joins = (held == target).astype(F32).astype(BF16)
    strips = [landed_ref[e, 24:48, :].astype(F32)[3:] for e in range(64)]
    ends = jnp.concatenate([p[18:] for p in strips], axis=0).astype(BF16)
    bias_ends = nn(joins, ends)
    for h in range(HEADS):
        main = jnp.concatenate([p[3 * h : 3 * h + 3] for p in strips], axis=0).astype(BF16)
        row = jnp.concatenate([nn(joins, main), bias_ends[:, 16 * h : 16 * h + 16]], axis=1)
        bias_full[h] = jnp.where(same, row, -jnp.inf)
        table_sum[h] = jnp.zeros((WIN, WIN), F32)
    gain_lane = lax.broadcasted_iota(jnp.int32, (8, 128), 1) - 96
    gain_lane = gain_lane == lax.broadcasted_iota(jnp.int32, (8, 128), 0)
    gain_lane = gain_lane.astype(F32).astype(BF16)
    gains = nt(gain_lane, ends)
    gain_sums[...] = jnp.zeros_like(gain_sums)
    rim = swap_quarters(rim_ref[...].astype(F32))
    natural = [swap_quarters(b[...].astype(F32)) for b in blocks]
    for k in range(4):
        ahead = jnp.where(last == k, rim, natural[k - 1])
        fore = jnp.concatenate([natural[k][6:], natural[k][:6]], axis=0)
        rear = jnp.concatenate([ahead[-6:], ahead[:-6]], axis=0)
        tokens[k] = jnp.where(is_left, fore, rear)
    gain_one = gains[0:1, :]
    gain_two = gains[1:2, :]
    lane = lax.broadcasted_iota(jnp.int32, (1, D), 1) // HEAD
    masks = [(lane == h).astype(BF16) for h in range(HEADS)]
    of_head = [slice(h * WIN, (h + 1) * WIN) for h in range(HEADS)]

    def own_lanes(stacked):
        out = stacked[of_head[0]]
        for h in range(1, HEADS):
            out = jnp.where(lane == h, stacked[of_head[h]], out)
        return out

    def one_window(w, carry):
        at = pl.multiple_of(w * WIN, 16)
        rows = pl.ds(at, WIN)
        both = tokens[w]
        cells = both[:, :D]
        cot = both[:, D:]
        cot_b = cot.astype(BF16)
        normed_one, inv_one = layer_norm(cells)
        scaled_one = (normed_one * gain_one).astype(BF16)
        s_one[rows, :] = scaled_one
        queries = nt(scaled_one, qkv_ref[0:D, :]).astype(BF16)
        key_rows = nt(scaled_one, qkv_ref[D : 2 * D, :]).astype(BF16)
        values = nt(scaled_one, qkv_ref[2 * D :, :]).astype(BF16)
        for h in range(HEADS):
            heads_q[of_head[h], :] = queries * masks[h]
        probs[...] = nt(heads_q[...], key_rows)
        for h in range(HEADS):
            scores = probs[of_head[h], :] * factor + bias_full[h]
            raised = jnp.exp(scores - jnp.max(scores, axis=-1, keepdims=True))
            p = raised * (1.0 / jnp.sum(raised, axis=-1, keepdims=True))
            probs[of_head[h], :] = p
            probs_b[of_head[h], :] = p.astype(BF16)
        attended = own_lanes(nn(probs_b[...], values))
        attended = attended.astype(BF16)
        att_all[rows, :] = attended
        middle = cells + nt(attended, proj_ref[...])
        normed_two, inv_two = layer_norm(middle)
        scaled_two = (normed_two * gain_two).astype(BF16)
        s_two[rows, :] = scaled_two
        d_htwo = jnp.zeros((WIN, D), F32)
        for c in range(3):
            part = slice(c * 256, (c + 1) * 256)
            pre_act = nt(scaled_two, up_ref[part, :])
            activated, slope = gelu_pair(pre_act)
            hid_all[rows, part] = activated.astype(BF16)
            d_hidden = (nn(cot_b, down_ref[:, part]) * slope).astype(BF16)
            dhid_all[rows, part] = d_hidden
            d_htwo = d_htwo + nn(d_hidden, up_ref[part, :])
        gain_sums[1:2, :] += jnp.sum(d_htwo * normed_two, axis=0, keepdims=True)
        d_middle = cot + norm_back(d_htwo * gain_two, normed_two, inv_two)
        d_middle_b = d_middle.astype(BF16)
        dmid_all[rows, :] = d_middle_b
        d_att = nn(d_middle_b, proj_ref[...]).astype(BF16)
        for h in range(HEADS):
            heads_d[of_head[h], :] = d_att * masks[h]
        d_probs[...] = nt(heads_d[...], values)
        for h in range(HEADS):
            p = probs[of_head[h], :]
            d_prob = d_probs[of_head[h], :]
            d_score = p * (d_prob - jnp.sum(p * d_prob, axis=-1, keepdims=True))
            table_sum[h] += d_score
            scores_b[of_head[h], :] = d_score.astype(BF16)
        d_queries = own_lanes(nn(scores_b[...], key_rows))
        d_keys = tn(scores_b[...], heads_q[...])
        d_values = tn(probs_b[...], heads_d[...])
        d_q = (d_queries * factor).astype(BF16)
        d_k = (d_keys * factor).astype(BF16)
        d_v = d_values.astype(BF16)
        dpack_all[0, rows, :] = d_q
        dpack_all[1, rows, :] = d_k
        dpack_all[2, rows, :] = d_v
        d_hone = (
            nn(d_q, qkv_ref[0:D, :]) + nn(d_k, qkv_ref[D : 2 * D, :]) + nn(d_v, qkv_ref[2 * D :, :])
        )
        gain_sums[0:1, :] += jnp.sum(d_hone * normed_one, axis=0, keepdims=True)
        d_tokens[w] = d_middle + norm_back(d_hone * gain_one, normed_one, inv_one)
        return carry

    lax.fori_loop(0, 4, one_window, 0, unroll=4)
    for k in range(4):
        mine, following = d_tokens[k], d_tokens[(k + 1) % 4]
        fore = jnp.concatenate([mine[-6:], mine[:-6]], axis=0)
        rear = jnp.concatenate([following[6:], following[:6]], axis=0)
        first = (k + 1) % 4 == last
        back_ref[k] = swap_quarters(
            jnp.where(is_left, jnp.where(first, 0.0, rear), fore)
        ).astype(BF16)

        @pl.when(first)
        def _():
            back_rim_ref[...] = swap_quarters(jnp.where(is_left, rear, 0.0)).astype(BF16)

    for part in range(3):
        g_qkv[part * D : (part + 1) * D, :] = tn(dpack_all[part], s_one[...])
    g_proj[...] = tn(dmid_all[...], att_all[...])
    cots = jnp.concatenate([tokens[k][:, D:] for k in range(4)], axis=0).astype(BF16)
    g_down[...] = tn(cots, hid_all[...])
    g_up[...] = tn(dhid_all[...], s_two[...])
    pack_grads(core_ref[0], g_qkv, g_proj, g_up, g_down, kept_ref, given_ref)
    spread_rows = [tn(joins, table_sum[h].astype(BF16)) for h in range(HEADS)]
    ends = jnp.concatenate([p[:, 128:] for p in spread_rows] + [jnp.zeros((192, 32), F32)], axis=1)
    ends = ends + tn(gain_sums[...].astype(BF16), gain_lane)
    for e in range(64):
        at = slice(3 * e, 3 * e + 3)
        piece = jnp.concatenate([p[at, :128] for p in spread_rows] + [ends[at]], axis=0)
        strips_ref[e] = piece.astype(BF16)


def block_grads(last, core, blocks, rim, halves, landed, row_label, col_label):
    rows = 4 * WIN
    out = [
        ((4, WIN, D), BF16),
        ((WIN, D), BF16),
        ((64, 27, 128), BF16),
        ((64, 27, 128), BF16),
        ((64, 21, 128), BF16),
    ]
    scratch = [
        ((3 * D, D), BF16),
        ((D, D), BF16),
        ((FFN, D), BF16),
        ((D, FFN), BF16),
        ((3 * D, D), F32),
        ((D, D), F32),
        ((FFN, D), F32),
        ((D, FFN), F32),
        ((4, WIN, 2 * D), F32),
        ((HEADS, WIN, WIN), F32),
        ((HEADS * WIN, WIN), F32),
        ((HEADS * WIN, WIN), F32),
        ((HEADS * WIN, WIN), BF16),
        ((HEADS * WIN, WIN), BF16),
        ((HEADS * WIN, D), BF16),
        ((HEADS * WIN, D), BF16),
        ((HEADS, WIN, WIN), F32),
        ((rows, D), BF16),
        ((rows, D), BF16),
        ((rows, D), BF16),
        ((rows, FFN), BF16),
        ((rows, FFN), BF16),
        ((rows, D), BF16),
        ((3, rows, D), BF16),
        ((4, WIN, D), F32),
        ((8, D), F32),
    ]
    whole = pl.BlockSpec(memory_space=pltpu.VMEM)
    return pl.pallas_call(
        block_kernel,
        in_specs=[pl.BlockSpec(memory_space=pltpu.SMEM)] * 2 + [whole] * 9,
        out_specs=[whole] * len(out),
        out_shape=[jax.ShapeDtypeStruct(s, t) for s, t in out],
        scratch_shapes=[pltpu.VMEM(s, t) for s, t in scratch],
        compiler_params=pltpu.CompilerParams(vmem_limit_bytes=48 << 20),
        name="block_grads",
    )(last.reshape(1), core.reshape(1), *blocks, rim, halves, landed, row_label, col_label)


def shards(
    inputs,
    cotangent,
    qkv_weight,
    proj_weight,
    up_weight,
    down_weight,
    norm_gains,
    bias_table,
    type_of,
    region,
):
    lat_index = lax.axis_index(LAT)
    core = lax.axis_index("core")
    x_index = lax.axis_index("x")
    type_count = bias_table.shape[0]
    positions = type_of.shape[0]
    own = bias_table.shape[2]
    groups = lax.axis_size("yl") * lax.axis_size("z")
    members = lax.axis_size("x")
    lons = groups * members

    cells = jnp.concatenate([inputs, cotangent], axis=-1)
    cells = jnp.roll(cells, -1, axis=0).reshape(positions, WPL, 2, WLAT // 2, WLON, 2 * D)
    cells = cells.transpose(0, 2, 1, 3, 4, 5).reshape(positions, 2, WIN // 2, 2 * D)

    rows = jnp.concatenate([qkv_weight.T, proj_weight.T], axis=0)
    rows = jnp.stack([up_weight.T.reshape(2, 6, D), rows.reshape(2, 6, D)], axis=1)
    ends = rows[..., 128:].reshape(2, 2, 2, 3, 64).transpose(0, 1, 3, 2, 4).reshape(2, 2, 3, 128)
    downs = down_weight.reshape(lons, 2, 6, 3).transpose(1, 3, 0, 2).reshape(2, 3, 3, 128)
    downs = downs.transpose(0, 2, 1, 3).reshape(2, 9, 128)
    both = jnp.concatenate([rows[..., :128], ends], axis=2)
    half = jnp.concatenate([both[:, 0], downs, both[:, 1]], axis=1)
    half = lax.dynamic_index_in_dim(half, core, 0, False)
    types = lax.dynamic_slice(type_of, (jnp.int32(0), lat_index), (positions, 1))[:, 0]
    onehot = types[:, None] == jnp.arange(type_count, dtype=jnp.int32)[None, :]
    slabs = jnp.dot(
        onehot.astype(BF16), bias_table.reshape(type_count, -1), preferred_element_type=F32
    ).astype(BF16)
    slabs = slabs.reshape(positions, HEADS, own)
    slabs = lax.dynamic_update_slice(
        jnp.zeros((positions, HEADS, 3 * WIN), BF16), slabs, (0, 0, x_index * 36)
    ).reshape(positions, HEADS, 3, WIN)
    main = slabs[..., :128].reshape(positions, 18, 128)
    ends = slabs[..., 128:].transpose(0, 2, 1, 3).reshape(positions, 3, 96)
    gain_part = jnp.broadcast_to(norm_gains.T[None], (positions, 3, 2))
    ends = jnp.concatenate([ends, gain_part, jnp.zeros((positions, 3, 30), BF16)], axis=2)
    slabs = jnp.concatenate([main, ends], axis=1)
    parcel = jnp.concatenate([jnp.broadcast_to(half[None], (positions, 27, 128)), slabs], axis=1)
    parcel = jnp.broadcast_to(parcel[None], (groups, members, 48, 128)).reshape(lons, 48, 128)

    arrived = passed_along(cells[:, 0], LAT, -1)
    parcel, arrived = lax.optimization_barrier((parcel, arrived))
    cells = jnp.concatenate([cells[:, 1], arrived], axis=1)
    cells = jnp.concatenate([cells, cells[: members - 1]], axis=0)
    cells = lax.dynamic_slice_in_dim(cells, x_index, members, 0)
    blocks = [cells[0]] + [passed_along(cells[k], ("x",), k) for k in range(1, members)]
    landed = lax.all_to_all(parcel, LON, 0, 0)
    is_first = [x_index == k for k in range(members)]
    rim = blocks[0]
    for k in range(1, members):
        rim = jnp.where(is_first[k], blocks[k], rim)
    rim = passed_along(rim, ("yl", "z"), -1)
    last = (x_index + 1) % members
    halves = lax.all_gather(landed[:, :27], "core", axis=0)

    labels = lax.dynamic_slice(region, (x_index * WPL, jnp.int32(0)), (WPL, WLAT))
    labels = jnp.broadcast_to(labels[:, :, None], (WPL, WLAT, WLON)).reshape(WIN)
    back, rim, kept, given, strips = block_grads(
        last, core, blocks, rim, halves, landed, labels.reshape(WIN, 1), labels.reshape(1, WIN)
    )

    g_half = kept.astype(F32) + passed_along(given, ("core",), 1).astype(F32)
    parcel = jnp.concatenate([g_half.astype(BF16), strips], axis=1)
    parcel, rim = lax.optimization_barrier((parcel, rim))
    rim = passed_along(rim, ("yl", "z"), 1)
    returned = lax.all_to_all(parcel, LON, 0, 0)
    blocks = [jnp.where(is_first[k], back[k] + rim, back[k]) for k in range(members)]
    blocks = [blocks[0]] + [passed_along(blocks[k], ("x",), -k) for k in range(1, members)]
    back = jnp.stack(blocks + blocks[: members - 1])
    back = lax.dynamic_slice_in_dim(back, (members - x_index) % members, members, 0)
    back = back.reshape(positions, 2, WIN // 2, D)
    arrived = passed_along(back[:, 1], LAT, 1)
    back = jnp.stack([arrived, back[:, 0]], axis=1)
    back = back.reshape(positions, 2, WPL, WLAT // 2, WLON, D).transpose(0, 2, 1, 3, 4, 5)
    grad_input = jnp.roll(back.reshape(inputs.shape), 1, axis=0)

    returned = returned.astype(F32)
    half_sum = jnp.sum(returned[:, :27], axis=0).reshape(-1)
    half_size = half_sum.shape[0]
    strip_sum = jnp.sum(returned[:, 27:].reshape(groups, members, 21, 128), axis=0)
    ends = strip_sum[:, 18:, :96].reshape(positions, 3, HEADS, 16).transpose(0, 2, 1, 3)
    table_part = jnp.concatenate(
        [strip_sum[:, :18].reshape(positions, HEADS, 3, 128), ends], axis=3
    ).reshape(positions, HEADS, 3 * WIN)
    table_part = lax.dynamic_slice_in_dim(table_part, x_index * 36, own, 2)
    gain_sum = jnp.sum(strip_sum[:, 18:, 96:98], axis=0).T.reshape(-1)
    note = jnp.concatenate([half_sum, table_part.reshape(-1), gain_sum])
    size = note.shape[0]
    note = jnp.pad(note.astype(BF16), (0, -size % 1024)).reshape(-1, 128)
    notes = lax.all_gather(note, LAT, axis=0).astype(F32).reshape(4, -1)
    whole = jnp.sum(notes[:, :half_size].reshape(2, 2, 27, 128), axis=0)
    table_size = positions * HEADS * own
    terms = notes[:, half_size : half_size + table_size].reshape(4 * positions, -1)
    gain_total = jnp.sum(notes[:, half_size + table_size : size], axis=0).reshape(2, 3)
    all_types = type_of.T.reshape(-1)
    select = jnp.arange(type_count, dtype=jnp.int32)[:, None] == all_types[None, :]
    grad_table = jnp.dot(select.astype(F32), terms, precision=lax.Precision.HIGHEST)
    factor = 1.0 / math.sqrt(inputs.shape[0] * inputs.shape[1] * inputs.shape[2] * 4 * lons)
    whole = whole * factor

    def joined(at):
        ends = whole[:, at + 6 : at + 9].reshape(2, 3, 2, 64).transpose(0, 2, 1, 3)
        rows = jnp.concatenate([whole[:, at : at + 6], ends.reshape(2, 6, 64)], axis=2)
        return rows.reshape(12, D)

    grad_up = joined(0).T
    rows = joined(18)
    grad_qkv = rows[:9].T
    grad_proj = rows[9:].T
    grad_down = whole[:, 9:18].reshape(2, 3, 3, 128).transpose(0, 2, 1, 3).reshape(2, 3, lons, 6)
    grad_down = grad_down.transpose(2, 0, 3, 1).reshape(FFN, 3)
    return (
        grad_input,
        grad_qkv,
        grad_proj,
        grad_up,
        grad_down,
        gain_total * factor,
        grad_table.reshape(type_count, HEADS, own),
    )


def solution(mesh):
    finer = Mesh(mesh.devices.reshape(2, 2, 2, 8, 4), ("yh", "core", "yl", "z", "x"))
    return jax.shard_map(
        shards,
        mesh=finer,
        in_specs=(
            P(None, LAT, LON, None),
            P(None, LAT, LON, None),
            P(None, LON),
            P(None, LON),
            P(None, LON),
            P(None, LON),
            P(None, LON),
            P(None, None, LON),
            P(),
            P(None, LAT),
        ),
        out_specs=(
            P(None, LAT, LON, None),
            P(None, LON),
            P(None, LON),
            P(None, LON),
            P(None, LON),
            P(None, LON),
            P(None, None, LON),
        ),
        check_vma=False,
    )
```

```python
import functools
import math

import jax
import jax.numpy as jnp
from jax import lax
from jax.experimental import pallas as pl
from jax.experimental.pallas import tpu as pltpu
from jax.sharding import Mesh, PartitionSpec as P

WPL = 2
WLAT = 6
WLON = 12
WIN = 144
D = 192
HEADS = 6
HEAD = 32
FFN = 768
LON = ("yl", "z", "x")
LAT = ("yh", "core")
F32 = jnp.float32
BF16 = jnp.bfloat16


def passed_along(block, axes, distance):
    size = math.prod(lax.axis_size(a) for a in axes)
    return lax.ppermute(block, axes, [((i - distance) % size, i) for i in range(size)])


def layer_norm(values):
    row_mean = jnp.mean(values, axis=-1, keepdims=True)
    centred = values - row_mean
    variance = jnp.mean(centred * centred, axis=-1, keepdims=True)
    inv_std = lax.rsqrt(variance + 1e-05)
    return (centred * inv_std, inv_std)


def norm_back(d_normed, normed, inv_std):
    return inv_std * (
        d_normed
        - jnp.mean(d_normed, axis=-1, keepdims=True)
        - normed * jnp.mean(d_normed * normed, axis=-1, keepdims=True)
    )


def gelu_pair(pre_act):
    cumul = 0.5 * (1.0 + lax.erf(pre_act * 0.7071067811865476))
    density = jnp.exp(-0.5 * pre_act * pre_act) * 0.3989422804014327
    return (pre_act * cumul, cumul + pre_act * density)


def spread(a, b, contract):
    return lax.dot_general(a, b, ((contract[0], contract[1]), ((), ())), preferred_element_type=F32)


def nt(a, b):
    return spread(a, b, ((1,), (1,)))


def nn(a, b):
    return spread(a, b, ((1,), (0,)))


def tn(a, b):
    return spread(a, b, ((0,), (0,)))


def swap_quarters(rows):
    return jnp.concatenate([rows[:36], rows[72:108], rows[36:72], rows[108:]], axis=0)


def unpack_weights(halves_ref, qkv_ref, proj_ref, up_ref, down_ref):
    def stack(pieces):
        return jnp.concatenate(pieces, axis=0).astype(BF16)

    for g in range(4):
        v = [[halves_ref[c, 16 * g + i].astype(F32) for i in range(16)] for c in range(2)]
        for c in range(2):
            rows = slice(c * 384 + 96 * g, c * 384 + 96 * (g + 1))
            up_ref[rows, :128] = stack([p[:6] for p in v[c]])
            up_ref[rows, 128:] = stack([p[6:9, s : s + 64] for p in v[c] for s in (0, 64)])
            for t in range(3):
                cols = slice(c * 384 + 128 * t, c * 384 + 128 * (t + 1))
                down_ref[48 * g : 48 * (g + 1), cols] = stack(
                    [p[9 + 3 * t : 12 + 3 * t] for p in v[c]]
                )
        rows = slice(144 * g, 144 * (g + 1))
        pairs = list(zip(v[0], v[1]))
        qkv_ref[rows, :128] = stack([q for a, b in pairs for q in (a[18:24], b[18:21])])
        qkv_ref[rows, 128:] = stack(
            [q for a, b in pairs for q in (a[24:27, :64], a[24:27, 64:], b[24:27, :64])]
        )
        rows = slice(48 * g, 48 * (g + 1))
        proj_ref[rows, :128] = stack([b[21:24] for b in v[1]])
        proj_ref[rows, 128:] = stack([b[24:27, 64:] for b in v[1]])


def pack_grads(core, g_qkv, g_proj, g_up, g_down, kept_ref, given_ref):
    def tails(ref, at, gap):
        return [ref[at : at + 3, 128:], ref[at + gap : at + gap + 3, 128:]]

    for e in range(64):
        pieces = []
        for c in range(2):
            at = c * 384 + 6 * e
            ups = [g_up[at : at + 6, :128], jnp.concatenate(tails(g_up, at, 3), axis=1)]
            downs = [
                g_down[3 * e : 3 * e + 3, c * 384 + 128 * t : c * 384 + 128 * (t + 1)]
                for t in range(3)
            ]
            if c == 0:
                rest = [g_qkv[9 * e : 9 * e + 6, :128]]
                ends = tails(g_qkv, 9 * e, 3)
            else:
                rest = [g_qkv[9 * e + 6 : 9 * e + 9, :128], g_proj[3 * e : 3 * e + 3, :128]]
                ends = [g_qkv[9 * e + 6 : 9 * e + 9, 128:], g_proj[3 * e : 3 * e + 3, 128:]]
            rest.append(jnp.concatenate(ends, axis=1))
            pieces.append(jnp.concatenate(ups + downs + rest, axis=0))
        kept_ref[e] = jnp.where(core == 0, pieces[0], pieces[1]).astype(BF16)
        given_ref[e] = jnp.where(core == 0, pieces[1], pieces[0]).astype(BF16)


def block_kernel(
    last_ref,
    core_ref,
    b0,
    b1,
    b2,
    b3,
    rim_ref,
    halves_ref,
    landed_ref,
    row_label_ref,
    col_label_ref,
    back_ref,
    back_rim_ref,
    kept_ref,
    given_ref,
    strips_ref,
    qkv_ref,
    proj_ref,
    up_ref,
    down_ref,
    g_qkv,
    g_proj,
    g_up,
    g_down,
    tokens,
    bias_full,
    probs,
    d_probs,
    probs_b,
    scores_b,
    heads_q,
    heads_d,
    table_sum,
    s_one,
    s_two,
    att_all,
    hid_all,
    dhid_all,
    dmid_all,
    dpack_all,
    d_tokens,
    gain_sums,
):
    factor = 1.0 / math.sqrt(HEAD)
    last = last_ref[0]
    blocks = (b0, b1, b2, b3)
    place = lax.broadcasted_iota(jnp.int32, (WIN, 1), 0) % WLON
    is_left = place < WLON // 2
    same = row_label_ref[...] == col_label_ref[...]
    unpack_weights(halves_ref, qkv_ref, proj_ref, up_ref, down_ref)
    source = lax.broadcasted_iota(jnp.int32, (WIN, 192), 1)
    target = lax.broadcasted_iota(jnp.int32, (WIN, 192), 0)
    held = 9 * (source // 12) + 2 * (source // 3 % 4) + source % 3
    joins = (held == target).astype(F32).astype(BF16)
    strips = [landed_ref[e, 24:48, :].astype(F32)[3:] for e in range(64)]
    ends = jnp.concatenate([p[18:] for p in strips], axis=0).astype(BF16)
    bias_ends = nn(joins, ends)
    for h in range(HEADS):
        main = jnp.concatenate([p[3 * h : 3 * h + 3] for p in strips], axis=0).astype(BF16)
        row = jnp.concatenate([nn(joins, main), bias_ends[:, 16 * h : 16 * h + 16]], axis=1)
        bias_full[h] = jnp.where(same, row, -jnp.inf)
        table_sum[h] = jnp.zeros((WIN, WIN), F32)
    gain_lane = lax.broadcasted_iota(jnp.int32, (8, 128), 1) - 96
    gain_lane = gain_lane == lax.broadcasted_iota(jnp.int32, (8, 128), 0)
    gain_lane = gain_lane.astype(F32).astype(BF16)
    gains = nt(gain_lane, ends)
    gain_sums[...] = jnp.zeros_like(gain_sums)
    rim = swap_quarters(rim_ref[...].astype(F32))
    natural = [swap_quarters(b[...].astype(F32)) for b in blocks]
    for k in range(4):
        ahead = jnp.where(last == k, rim, natural[k - 1])
        fore = jnp.concatenate([natural[k][6:], natural[k][:6]], axis=0)
        rear = jnp.concatenate([ahead[-6:], ahead[:-6]], axis=0)
        tokens[k] = jnp.where(is_left, fore, rear)
    gain_one = gains[0:1, :]
    gain_two = gains[1:2, :]
    lane = lax.broadcasted_iota(jnp.int32, (1, D), 1) // HEAD
    masks = [(lane == h).astype(BF16) for h in range(HEADS)]
    of_head = [slice(h * WIN, (h + 1) * WIN) for h in range(HEADS)]

    def own_lanes(stacked):
        out = stacked[of_head[0]]
        for h in range(1, HEADS):
            out = jnp.where(lane == h, stacked[of_head[h]], out)
        return out

    def one_window(w, carry):
        at = pl.multiple_of(w * WIN, 16)
        rows = pl.ds(at, WIN)
        both = tokens[w]
        cells = both[:, :D]
        cot = both[:, D:]
        cot_b = cot.astype(BF16)
        normed_one, inv_one = layer_norm(cells)
        scaled_one = (normed_one * gain_one).astype(BF16)
        s_one[rows, :] = scaled_one
        queries = nt(scaled_one, qkv_ref[0:D, :]).astype(BF16)
        key_rows = nt(scaled_one, qkv_ref[D : 2 * D, :]).astype(BF16)
        values = nt(scaled_one, qkv_ref[2 * D :, :]).astype(BF16)
        for h in range(HEADS):
            heads_q[of_head[h], :] = queries * masks[h]
        probs[...] = nt(heads_q[...], key_rows)
        for h in range(HEADS):
            scores = probs[of_head[h], :] * factor + bias_full[h]
            raised = jnp.exp(scores - jnp.max(scores, axis=-1, keepdims=True))
            p = raised * (1.0 / jnp.sum(raised, axis=-1, keepdims=True))
            probs[of_head[h], :] = p
            probs_b[of_head[h], :] = p.astype(BF16)
        attended = own_lanes(nn(probs_b[...], values))
        attended = attended.astype(BF16)
        att_all[rows, :] = attended
        middle = cells + nt(attended, proj_ref[...])
        normed_two, inv_two = layer_norm(middle)
        scaled_two = (normed_two * gain_two).astype(BF16)
        s_two[rows, :] = scaled_two
        d_htwo = jnp.zeros((WIN, D), F32)
        for c in range(3):
            part = slice(c * 256, (c + 1) * 256)
            pre_act = nt(scaled_two, up_ref[part, :])
            activated, slope = gelu_pair(pre_act)
            hid_all[rows, part] = activated.astype(BF16)
            d_hidden = (nn(cot_b, down_ref[:, part]) * slope).astype(BF16)
            dhid_all[rows, part] = d_hidden
            d_htwo = d_htwo + nn(d_hidden, up_ref[part, :])
        gain_sums[1:2, :] += jnp.sum(d_htwo * normed_two, axis=0, keepdims=True)
        d_middle = cot + norm_back(d_htwo * gain_two, normed_two, inv_two)
        d_middle_b = d_middle.astype(BF16)
        dmid_all[rows, :] = d_middle_b
        d_att = nn(d_middle_b, proj_ref[...]).astype(BF16)
        for h in range(HEADS):
            heads_d[of_head[h], :] = d_att * masks[h]
        d_probs[...] = nt(heads_d[...], values)
        for h in range(HEADS):
            p = probs[of_head[h], :]
            d_prob = d_probs[of_head[h], :]
            d_score = p * (d_prob - jnp.sum(p * d_prob, axis=-1, keepdims=True))
            table_sum[h] += d_score
            scores_b[of_head[h], :] = d_score.astype(BF16)
        d_queries = own_lanes(nn(scores_b[...], key_rows))
        d_keys = tn(scores_b[...], heads_q[...])
        d_values = tn(probs_b[...], heads_d[...])
        d_q = (d_queries * factor).astype(BF16)
        d_k = (d_keys * factor).astype(BF16)
        d_v = d_values.astype(BF16)
        dpack_all[0, rows, :] = d_q
        dpack_all[1, rows, :] = d_k
        dpack_all[2, rows, :] = d_v
        d_hone = (
            nn(d_q, qkv_ref[0:D, :]) + nn(d_k, qkv_ref[D : 2 * D, :]) + nn(d_v, qkv_ref[2 * D :, :])
        )
        gain_sums[0:1, :] += jnp.sum(d_hone * normed_one, axis=0, keepdims=True)
        d_tokens[w] = d_middle + norm_back(d_hone * gain_one, normed_one, inv_one)
        return carry

    lax.fori_loop(0, 4, one_window, 0, unroll=4)
    for k in range(4):
        mine, following = d_tokens[k], d_tokens[(k + 1) % 4]
        fore = jnp.concatenate([mine[-6:], mine[:-6]], axis=0)
        rear = jnp.concatenate([following[6:], following[:6]], axis=0)
        first = (k + 1) % 4 == last
        back_ref[k] = swap_quarters(
            jnp.where(is_left, jnp.where(first, 0.0, rear), fore)
        ).astype(BF16)

        @pl.when(first)
        def _():
            back_rim_ref[...] = swap_quarters(jnp.where(is_left, rear, 0.0)).astype(BF16)

    for part in range(3):
        g_qkv[part * D : (part + 1) * D, :] = tn(dpack_all[part], s_one[...])
    g_proj[...] = tn(dmid_all[...], att_all[...])
    cots = jnp.concatenate([tokens[k][:, D:] for k in range(4)], axis=0).astype(BF16)
    g_down[...] = tn(cots, hid_all[...])
    g_up[...] = tn(dhid_all[...], s_two[...])
    pack_grads(core_ref[0], g_qkv, g_proj, g_up, g_down, kept_ref, given_ref)
    spread_rows = [tn(joins, table_sum[h].astype(BF16)) for h in range(HEADS)]
    ends = jnp.concatenate([p[:, 128:] for p in spread_rows] + [jnp.zeros((192, 32), F32)], axis=1)
    ends = ends + tn(gain_sums[...].astype(BF16), gain_lane)
    for e in range(64):
        at = slice(3 * e, 3 * e + 3)
        piece = jnp.concatenate([p[at, :128] for p in spread_rows] + [ends[at]], axis=0)
        strips_ref[e] = piece.astype(BF16)


def block_grads(last, core, blocks, rim, halves, landed, row_label, col_label):
    rows = 4 * WIN
    out = [
        ((4, WIN, D), BF16),
        ((WIN, D), BF16),
        ((64, 27, 128), BF16),
        ((64, 27, 128), BF16),
        ((64, 21, 128), BF16),
    ]
    scratch = [
        ((3 * D, D), BF16),
        ((D, D), BF16),
        ((FFN, D), BF16),
        ((D, FFN), BF16),
        ((3 * D, D), F32),
        ((D, D), F32),
        ((FFN, D), F32),
        ((D, FFN), F32),
        ((4, WIN, 2 * D), F32),
        ((HEADS, WIN, WIN), F32),
        ((HEADS * WIN, WIN), F32),
        ((HEADS * WIN, WIN), F32),
        ((HEADS * WIN, WIN), BF16),
        ((HEADS * WIN, WIN), BF16),
        ((HEADS * WIN, D), BF16),
        ((HEADS * WIN, D), BF16),
        ((HEADS, WIN, WIN), F32),
        ((rows, D), BF16),
        ((rows, D), BF16),
        ((rows, D), BF16),
        ((rows, FFN), BF16),
        ((rows, FFN), BF16),
        ((rows, D), BF16),
        ((3, rows, D), BF16),
        ((4, WIN, D), F32),
        ((8, D), F32),
    ]
    whole = pl.BlockSpec(memory_space=pltpu.VMEM)
    return pl.pallas_call(
        block_kernel,
        in_specs=[pl.BlockSpec(memory_space=pltpu.SMEM)] * 2 + [whole] * 9,
        out_specs=[whole] * len(out),
        out_shape=[jax.ShapeDtypeStruct(s, t) for s, t in out],
        scratch_shapes=[pltpu.VMEM(s, t) for s, t in scratch],
        compiler_params=pltpu.CompilerParams(vmem_limit_bytes=48 << 20),
        name="block_grads",
    )(last.reshape(1), core.reshape(1), *blocks, rim, halves, landed, row_label, col_label)


def one_hot(mask):
    return mask.astype(F32).astype(BF16)


def iota2(shape, axis):
    return lax.broadcasted_iota(jnp.int32, shape, axis)


def pack_kernel(
    spot_ref, types_ref, qkv_ref, proj_ref, up_ref, down_ref, gains_ref, table_ref, out_ref
):
    x_index, core, lat = spot_ref[0], spot_ref[1], spot_ref[2]

    first = up_ref[...].astype(F32)
    second = jnp.concatenate([qkv_ref[...].astype(F32), proj_ref[...].astype(F32)], axis=0)
    halves = []
    for rows in (first, second):
        rows = jnp.where(core == 0, rows[:6], rows[6:])
        halves.append(rows[:, :128])
        halves.append(jnp.concatenate([rows[:3, 128:], rows[3:, 128:]], axis=1))
    unit = iota2((1, 384), 1)
    unit = 12 * (unit // 6) + unit % 6 + 6 * core
    chosen = one_hot(iota2((FFN, 384), 0) == unit)
    downs = nn(down_ref[...], chosen)
    downs = [downs[:, 128 * t : 128 * (t + 1)] for t in range(3)]
    half = halves[:2] + downs + halves[2:]
    spots = one_hot(iota2((2, 128), 1) == 96 + iota2((2, 128), 0))
    gain_ends = tn(gains_ref[...], spots)
    wanted = jnp.full((8, 16), -1, jnp.int32)
    for a in range(4):
        wanted = jnp.where(iota2((8, 16), 0) == a, types_ref[a, lat], wanted)
    wanted = one_hot(iota2((8, 16), 1) == wanted)
    slabs = []
    for h in range(HEADS):
        slab = nn(wanted, table_ref[h])
        slab = jnp.concatenate([slab, jnp.zeros((8, 512 - 324), F32)], axis=1)
        slabs.append(pltpu.roll(slab, x_index * 36, 1))
    for a in range(4):
        slab = jnp.concatenate([p[a : a + 1] for p in slabs], axis=0)
        mains = [slab[:, WIN * r : WIN * r + 128] for r in range(3)]
        mains = [m[h : h + 1] for h in range(HEADS) for m in mains]
        ends = []
        for r in range(3):
            end = slab[:, WIN * r + 128 : WIN * (r + 1)]
            ends.append(jnp.concatenate([end[h : h + 1] for h in range(HEADS)], axis=1))
        ends = jnp.concatenate([jnp.concatenate(ends, axis=0), jnp.zeros((3, 32), F32)], axis=1)
        piece = jnp.concatenate(half + mains + [ends + gain_ends], axis=0).astype(BF16)
        for g in range(16):
            out_ref[4 * g + a] = piece


def finish_kernel(
    factor, types_ref, notes_ref, qkv_ref, proj_ref, up_ref, down_ref, gains_ref, table_ref
):
    notes = [notes_ref[i, :32, :].astype(F32) for i in range(4)]

    def six(note, at):
        ends = [note[at + 6 : at + 9, :64], note[at + 6 : at + 9, 64:]]
        return jnp.concatenate([note[at : at + 6], jnp.concatenate(ends, axis=0)], axis=1)

    sums = [(notes[c] + notes[2 + c]) * factor for c in range(2)]
    up_ref[:6, :] = six(sums[0], 0)
    up_ref[6:, :] = six(sums[1], 0)
    rest = six(sums[1], 18)
    qkv_ref[:6, :] = six(sums[0], 18)
    qkv_ref[6:, :] = rest[:3]
    proj_ref[...] = rest[3:]
    unit = iota2((1, 384), 1)
    unit = 12 * (unit // 6) + unit % 6
    downs = jnp.zeros((3, FFN), F32)
    for c in range(2):
        parts = []
        for note in (notes[c], notes[2 + c]):
            parts.append(
                jnp.concatenate([note[9 + 3 * t : 12 + 3 * t] for t in range(3)], axis=1)
            )
        parts = jnp.concatenate(parts, axis=0).astype(BF16)
        placed = nt(parts, one_hot(iota2((FFN, 384), 0) == unit + 6 * c))
        downs = downs + (placed[:3] + placed[3:])
    down_ref[...] = downs * factor
    gains = (notes[0] + notes[1] + notes[2] + notes[3])[27:28] * factor
    gains_ref[0:1, :] = gains[:, :3]
    gains_ref[1:2, :] = gains[:, 3:6]
    wanted = jnp.zeros((16, 16), jnp.int32)
    for i in range(4):
        for a in range(4):
            wanted = jnp.where(iota2((16, 16), 1) == 4 * i + a, types_ref[a, i], wanted)
    wanted = one_hot(iota2((16, 16), 0) == wanted)
    tables = [notes_ref[i, 32:104, :].astype(F32) for i in range(4)]
    for h in range(HEADS):
        lanes = []
        for j in range(3):
            at = 4 * (3 * h + j)
            terms = jnp.concatenate([t[at : at + 4] for t in tables], axis=0).astype(BF16)
            lanes.append(nn(wanted, terms))
        table_ref[h] = jnp.concatenate(lanes, axis=1)[:, :324]


def small_call(kernel, args, scalars, out, scratch, name):
    whole = pl.BlockSpec(memory_space=pltpu.VMEM)
    flat = pl.BlockSpec(memory_space=pltpu.SMEM)
    return pl.pallas_call(
        kernel,
        in_specs=[flat] * scalars + [whole] * (len(args) - scalars),
        out_specs=[whole] * len(out),
        out_shape=[jax.ShapeDtypeStruct(s, t) for s, t in out],
        scratch_shapes=[pltpu.VMEM(s, t) for s, t in scratch],
        name=name,
    )(*args)


def shards(
    inputs,
    cotangent,
    qkv_weight,
    proj_weight,
    up_weight,
    down_weight,
    norm_gains,
    bias_table,
    type_of,
    region,
):
    lat_index = lax.axis_index(LAT)
    core = lax.axis_index("core")
    x_index = lax.axis_index("x")
    type_count = bias_table.shape[0]
    positions = type_of.shape[0]
    own = bias_table.shape[2]
    groups = lax.axis_size("yl") * lax.axis_size("z")
    members = lax.axis_size("x")
    lons = groups * members

    cells = jnp.concatenate([inputs, cotangent], axis=-1)
    cells = jnp.roll(cells, -1, axis=0).reshape(positions, WPL, 2, WLAT // 2, WLON, 2 * D)
    cells = cells.transpose(0, 2, 1, 3, 4, 5).reshape(positions, 2, WIN // 2, 2 * D)

    spot = jnp.stack([x_index, core, lat_index]).astype(jnp.int32)
    weights = [w.T for w in (qkv_weight, proj_weight, up_weight, down_weight)]
    weights += [norm_gains, bias_table.transpose(1, 0, 2)]
    (parcel,) = small_call(
        pack_kernel, (spot, type_of, *weights), 2, [((lons, 48, 128), BF16)], [], "pack"
    )

    arrived = passed_along(cells[:, 0], LAT, -1)
    parcel, arrived = lax.optimization_barrier((parcel, arrived))
    cells = jnp.concatenate([cells[:, 1], arrived], axis=1)
    cells = jnp.concatenate([cells, cells[: members - 1]], axis=0)
    cells = lax.dynamic_slice_in_dim(cells, x_index, members, 0)
    blocks = [cells[0]] + [passed_along(cells[k], ("x",), k) for k in range(1, members)]
    landed = lax.all_to_all(parcel, LON, 0, 0)
    is_first = [x_index == k for k in range(members)]
    rim = blocks[0]
    for k in range(1, members):
        rim = jnp.where(is_first[k], blocks[k], rim)
    rim = passed_along(rim, ("yl", "z"), -1)
    last = (x_index + 1) % members
    halves = lax.all_gather(landed[:, :27], "core", axis=0)

    labels = lax.dynamic_slice(region, (x_index * WPL, jnp.int32(0)), (WPL, WLAT))
    labels = jnp.broadcast_to(labels[:, :, None], (WPL, WLAT, WLON)).reshape(WIN)
    back, rim, kept, given, strips = block_grads(
        last, core, blocks, rim, halves, landed, labels.reshape(WIN, 1), labels.reshape(1, WIN)
    )

    g_half = kept.astype(F32) + passed_along(given, ("core",), 1).astype(F32)
    parcel = jnp.concatenate([g_half.astype(BF16), strips], axis=1)
    parcel, rim = lax.optimization_barrier((parcel, rim))
    rim = passed_along(rim, ("yl", "z"), 1)
    returned = lax.all_to_all(parcel, LON, 0, 0)
    blocks = [jnp.where(is_first[k], back[k] + rim, back[k]) for k in range(members)]
    blocks = [blocks[0]] + [passed_along(blocks[k], ("x",), -k) for k in range(1, members)]
    back = jnp.stack(blocks + blocks[: members - 1])
    back = lax.dynamic_slice_in_dim(back, (members - x_index) % members, members, 0)
    back = back.reshape(positions, 2, WIN // 2, D)
    arrived = passed_along(back[:, 1], LAT, 1)
    back = jnp.stack([arrived, back[:, 0]], axis=1)
    back = back.reshape(positions, 2, WPL, WLAT // 2, WLON, D).transpose(0, 2, 1, 3, 4, 5)
    grad_input = jnp.roll(back.reshape(inputs.shape), 1, axis=0)

    returned = returned.astype(F32)
    half_sum = jnp.sum(returned[:, :27], axis=0)
    strip_sum = jnp.sum(returned[:, 27:].reshape(groups, members, 21, 128), axis=0)
    ends = strip_sum[:, 18:, :96].reshape(positions, 3, HEADS, 16).transpose(0, 2, 1, 3)
    table_part = jnp.concatenate(
        [strip_sum[:, :18].reshape(positions, HEADS, 3, 128), ends], axis=3
    ).reshape(positions, HEADS, 3 * WIN)
    table_part = lax.dynamic_slice_in_dim(table_part, x_index * 36, own, 2)
    gain_sum = jnp.sum(strip_sum[:, 18:, 96:98], axis=0).T.reshape(-1)
    note = jnp.pad(table_part, ((0, 0), (0, 0), (0, 384 - own))).reshape(positions, 18, 128)
    note = note.transpose(1, 0, 2).reshape(72, 128)
    gain_row = jnp.pad(gain_sum.reshape(1, 6), ((0, 4), (0, 122)))
    note = jnp.concatenate([half_sum, gain_row, note], axis=0).astype(BF16)
    notes = lax.all_gather(note, LAT, axis=0)
    factor = 1.0 / math.sqrt(inputs.shape[0] * inputs.shape[1] * inputs.shape[2] * 4 * lons)
    shapes = [w.shape[::-1] for w in (qkv_weight, proj_weight, up_weight, down_weight)]
    shapes += [norm_gains.shape, (HEADS, type_count, own)]
    out = [(shape, F32) for shape in shapes]
    kernel = functools.partial(finish_kernel, factor)
    grads = small_call(kernel, (type_of, notes), 1, out, [], "finish")
    table = grads[5].transpose(1, 0, 2)
    return (grad_input, grads[0].T, grads[1].T, grads[2].T, grads[3].T, grads[4], table)


def solution(mesh):
    finer = Mesh(mesh.devices.reshape(2, 2, 2, 8, 4), ("yh", "core", "yl", "z", "x"))
    return jax.shard_map(
        shards,
        mesh=finer,
        in_specs=(
            P(None, LAT, LON, None),
            P(None, LAT, LON, None),
            P(None, LON),
            P(None, LON),
            P(None, LON),
            P(None, LON),
            P(None, LON),
            P(None, None, LON),
            P(),
            P(None, LAT),
        ),
        out_specs=(
            P(None, LAT, LON, None),
            P(None, LON),
            P(None, LON),
            P(None, LON),
            P(None, LON),
            P(None, LON),
            P(None, None, LON),
        ),
        check_vma=False,
    )
```

```python
import functools
import math

import jax
import jax.numpy as jnp
from jax import lax
from jax.experimental import pallas as pl
from jax.experimental.pallas import tpu as pltpu
from jax.sharding import Mesh, PartitionSpec as P

WPL = 2
WLAT = 6
WLON = 12
WIN = 144
D = 192
HEADS = 6
HEAD = 32
FFN = 768
LON = ("yl", "z", "x")
LAT = ("yh", "core")
F32 = jnp.float32
BF16 = jnp.bfloat16


def passed_along(block, axes, distance):
    size = math.prod(lax.axis_size(a) for a in axes)
    return lax.ppermute(block, axes, [((i - distance) % size, i) for i in range(size)])


def layer_norm(values):
    row_mean = jnp.mean(values, axis=-1, keepdims=True)
    centred = values - row_mean
    variance = jnp.mean(centred * centred, axis=-1, keepdims=True)
    inv_std = lax.rsqrt(variance + 1e-05)
    return (centred * inv_std, inv_std)


def norm_back(d_normed, normed, inv_std):
    return inv_std * (
        d_normed
        - jnp.mean(d_normed, axis=-1, keepdims=True)
        - normed * jnp.mean(d_normed * normed, axis=-1, keepdims=True)
    )


def gelu_pair(pre_act):
    cumul = 0.5 * (1.0 + lax.erf(pre_act * 0.7071067811865476))
    density = jnp.exp(-0.5 * pre_act * pre_act) * 0.3989422804014327
    return (pre_act * cumul, cumul + pre_act * density)


def spread(a, b, contract):
    return lax.dot_general(a, b, ((contract[0], contract[1]), ((), ())), preferred_element_type=F32)


def nt(a, b):
    return spread(a, b, ((1,), (1,)))


def nn(a, b):
    return spread(a, b, ((1,), (0,)))


def tn(a, b):
    return spread(a, b, ((0,), (0,)))


def swap_quarters(rows):
    return jnp.concatenate([rows[:36], rows[72:108], rows[36:72], rows[108:]], axis=0)


def unpack_weights(core, mine_ref, other_ref, qkv_ref, proj_ref, up_ref, down_ref):
    def stack(pieces):
        return jnp.concatenate(pieces, axis=0).astype(BF16)

    for g in range(4):
        mine = [mine_ref[16 * g + i, :32, :].astype(F32)[:27] for i in range(16)]
        other = [other_ref[16 * g + i, :32, :].astype(F32)[:27] for i in range(16)]
        v = [
            [jnp.where(core == c, a, b) for a, b in zip(mine, other)] for c in range(2)
        ]
        for c in range(2):
            rows = slice(c * 384 + 96 * g, c * 384 + 96 * (g + 1))
            up_ref[rows, :128] = stack([p[:6] for p in v[c]])
            up_ref[rows, 128:] = stack([p[6:9, s : s + 64] for p in v[c] for s in (0, 64)])
            for t in range(3):
                cols = slice(c * 384 + 128 * t, c * 384 + 128 * (t + 1))
                down_ref[48 * g : 48 * (g + 1), cols] = stack(
                    [p[9 + 3 * t : 12 + 3 * t] for p in v[c]]
                )
        rows = slice(144 * g, 144 * (g + 1))
        pairs = list(zip(v[0], v[1]))
        qkv_ref[rows, :128] = stack([q for a, b in pairs for q in (a[18:24], b[18:21])])
        qkv_ref[rows, 128:] = stack(
            [q for a, b in pairs for q in (a[24:27, :64], a[24:27, 64:], b[24:27, :64])]
        )
        rows = slice(48 * g, 48 * (g + 1))
        proj_ref[rows, :128] = stack([b[21:24] for b in v[1]])
        proj_ref[rows, 128:] = stack([b[24:27, 64:] for b in v[1]])


def pack_grads(core, g_qkv, g_proj, g_up, g_down, kept_ref, given_ref):
    def tails(ref, at, gap):
        return [ref[at : at + 3, 128:], ref[at + gap : at + gap + 3, 128:]]

    for e in range(64):
        pieces = []
        for c in range(2):
            at = c * 384 + 6 * e
            ups = [g_up[at : at + 6, :128], jnp.concatenate(tails(g_up, at, 3), axis=1)]
            downs = [
                g_down[3 * e : 3 * e + 3, c * 384 + 128 * t : c * 384 + 128 * (t + 1)]
                for t in range(3)
            ]
            if c == 0:
                rest = [g_qkv[9 * e : 9 * e + 6, :128]]
                ends = tails(g_qkv, 9 * e, 3)
            else:
                rest = [g_qkv[9 * e + 6 : 9 * e + 9, :128], g_proj[3 * e : 3 * e + 3, :128]]
                ends = [g_qkv[9 * e + 6 : 9 * e + 9, 128:], g_proj[3 * e : 3 * e + 3, 128:]]
            rest.append(jnp.concatenate(ends, axis=1))
            pieces.append(jnp.concatenate(ups + downs + rest, axis=0))
        kept_ref[e] = jnp.where(core == 0, pieces[0], pieces[1]).astype(BF16)
        given_ref[e] = jnp.where(core == 0, pieces[1], pieces[0]).astype(BF16)


def block_kernel(
    last_ref,
    core_ref,
    b0,
    b1,
    b2,
    b3,
    rim_ref,
    halves_ref,
    landed_ref,
    row_label_ref,
    col_label_ref,
    back_ref,
    back_rim_ref,
    kept_ref,
    given_ref,
    strips_ref,
    qkv_ref,
    proj_ref,
    up_ref,
    down_ref,
    g_qkv,
    g_proj,
    g_up,
    g_down,
    tokens,
    bias_full,
    probs,
    d_probs,
    probs_b,
    scores_b,
    heads_q,
    heads_d,
    table_sum,
    s_one,
    s_two,
    att_all,
    hid_all,
    dhid_all,
    dmid_all,
    dpack_all,
    d_tokens,
    gain_sums,
):
    factor = 1.0 / math.sqrt(HEAD)
    last = last_ref[0]
    blocks = (b0, b1, b2, b3)
    place = lax.broadcasted_iota(jnp.int32, (WIN, 1), 0) % WLON
    is_left = place < WLON // 2
    same = row_label_ref[...] == col_label_ref[...]
    unpack_weights(core_ref[0], landed_ref, halves_ref, qkv_ref, proj_ref, up_ref, down_ref)
    source = lax.broadcasted_iota(jnp.int32, (WIN, 192), 1)
    target = lax.broadcasted_iota(jnp.int32, (WIN, 192), 0)
    held = 9 * (source // 12) + 2 * (source // 3 % 4) + source % 3
    joins = (held == target).astype(F32).astype(BF16)
    strips = [landed_ref[e, 24:48, :].astype(F32)[3:] for e in range(64)]
    ends = jnp.concatenate([p[18:] for p in strips], axis=0).astype(BF16)
    bias_ends = nn(joins, ends)
    for h in range(HEADS):
        main = jnp.concatenate([p[3 * h : 3 * h + 3] for p in strips], axis=0).astype(BF16)
        row = jnp.concatenate([nn(joins, main), bias_ends[:, 16 * h : 16 * h + 16]], axis=1)
        bias_full[h] = jnp.where(same, row, -jnp.inf)
        table_sum[h] = jnp.zeros((WIN, WIN), F32)
    gain_lane = lax.broadcasted_iota(jnp.int32, (8, 128), 1) - 96
    gain_lane = gain_lane == lax.broadcasted_iota(jnp.int32, (8, 128), 0)
    gain_lane = gain_lane.astype(F32).astype(BF16)
    gains = nt(gain_lane, ends)
    gain_sums[...] = jnp.zeros_like(gain_sums)
    rim = swap_quarters(rim_ref[...].astype(F32))
    natural = [swap_quarters(b[...].astype(F32)) for b in blocks]
    for k in range(4):
        ahead = jnp.where(last == k, rim, natural[k - 1])
        fore = jnp.concatenate([natural[k][6:], natural[k][:6]], axis=0)
        rear = jnp.concatenate([ahead[-6:], ahead[:-6]], axis=0)
        tokens[k] = jnp.where(is_left, fore, rear)
    gain_one = gains[0:1, :]
    gain_two = gains[1:2, :]
    lane = lax.broadcasted_iota(jnp.int32, (1, D), 1) // HEAD
    masks = [(lane == h).astype(BF16) for h in range(HEADS)]
    of_head = [slice(h * WIN, (h + 1) * WIN) for h in range(HEADS)]

    def own_lanes(stacked):
        out = stacked[of_head[0]]
        for h in range(1, HEADS):
            out = jnp.where(lane == h, stacked[of_head[h]], out)
        return out

    def one_window(w, carry):
        at = pl.multiple_of(w * WIN, 16)
        rows = pl.ds(at, WIN)
        both = tokens[w]
        cells = both[:, :D]
        cot = both[:, D:]
        cot_b = cot.astype(BF16)
        normed_one, inv_one = layer_norm(cells)
        scaled_one = (normed_one * gain_one).astype(BF16)
        s_one[rows, :] = scaled_one
        queries = nt(scaled_one, qkv_ref[0:D, :]).astype(BF16)
        key_rows = nt(scaled_one, qkv_ref[D : 2 * D, :]).astype(BF16)
        values = nt(scaled_one, qkv_ref[2 * D :, :]).astype(BF16)
        for h in range(HEADS):
            heads_q[of_head[h], :] = queries * masks[h]
        probs[...] = nt(heads_q[...], key_rows)
        for h in range(HEADS):
            scores = probs[of_head[h], :] * factor + bias_full[h]
            raised = jnp.exp(scores - jnp.max(scores, axis=-1, keepdims=True))
            p = raised * (1.0 / jnp.sum(raised, axis=-1, keepdims=True))
            probs[of_head[h], :] = p
            probs_b[of_head[h], :] = p.astype(BF16)
        attended = own_lanes(nn(probs_b[...], values))
        attended = attended.astype(BF16)
        att_all[rows, :] = attended
        middle = cells + nt(attended, proj_ref[...])
        normed_two, inv_two = layer_norm(middle)
        scaled_two = (normed_two * gain_two).astype(BF16)
        s_two[rows, :] = scaled_two
        d_htwo = jnp.zeros((WIN, D), F32)
        for c in range(3):
            part = slice(c * 256, (c + 1) * 256)
            pre_act = nt(scaled_two, up_ref[part, :])
            activated, slope = gelu_pair(pre_act)
            hid_all[rows, part] = activated.astype(BF16)
            d_hidden = (nn(cot_b, down_ref[:, part]) * slope).astype(BF16)
            dhid_all[rows, part] = d_hidden
            d_htwo = d_htwo + nn(d_hidden, up_ref[part, :])
        gain_sums[1:2, :] += jnp.sum(d_htwo * normed_two, axis=0, keepdims=True)
        d_middle = cot + norm_back(d_htwo * gain_two, normed_two, inv_two)
        d_middle_b = d_middle.astype(BF16)
        dmid_all[rows, :] = d_middle_b
        d_att = nn(d_middle_b, proj_ref[...]).astype(BF16)
        for h in range(HEADS):
            heads_d[of_head[h], :] = d_att * masks[h]
        d_probs[...] = nt(heads_d[...], values)
        for h in range(HEADS):
            p = probs[of_head[h], :]
            d_prob = d_probs[of_head[h], :]
            d_score = p * (d_prob - jnp.sum(p * d_prob, axis=-1, keepdims=True))
            table_sum[h] += d_score
            scores_b[of_head[h], :] = d_score.astype(BF16)
        d_queries = own_lanes(nn(scores_b[...], key_rows))
        d_keys = tn(scores_b[...], heads_q[...])
        d_values = tn(probs_b[...], heads_d[...])
        d_q = (d_queries * factor).astype(BF16)
        d_k = (d_keys * factor).astype(BF16)
        d_v = d_values.astype(BF16)
        dpack_all[0, rows, :] = d_q
        dpack_all[1, rows, :] = d_k
        dpack_all[2, rows, :] = d_v
        d_hone = (
            nn(d_q, qkv_ref[0:D, :]) + nn(d_k, qkv_ref[D : 2 * D, :]) + nn(d_v, qkv_ref[2 * D :, :])
        )
        gain_sums[0:1, :] += jnp.sum(d_hone * normed_one, axis=0, keepdims=True)
        d_tokens[w] = d_middle + norm_back(d_hone * gain_one, normed_one, inv_one)
        return carry

    lax.fori_loop(0, 4, one_window, 0, unroll=4)
    for k in range(4):
        mine, following = d_tokens[k], d_tokens[(k + 1) % 4]
        fore = jnp.concatenate([mine[-6:], mine[:-6]], axis=0)
        rear = jnp.concatenate([following[6:], following[:6]], axis=0)
        first = (k + 1) % 4 == last
        back_ref[k] = swap_quarters(
            jnp.where(is_left, jnp.where(first, 0.0, rear), fore)
        ).astype(BF16)

        @pl.when(first)
        def _():
            back_rim_ref[...] = swap_quarters(jnp.where(is_left, rear, 0.0)).astype(BF16)

    for part in range(3):
        g_qkv[part * D : (part + 1) * D, :] = tn(dpack_all[part], s_one[...])
    g_proj[...] = tn(dmid_all[...], att_all[...])
    cots = jnp.concatenate([tokens[k][:, D:] for k in range(4)], axis=0).astype(BF16)
    g_down[...] = tn(cots, hid_all[...])
    g_up[...] = tn(dhid_all[...], s_two[...])
    pack_grads(core_ref[0], g_qkv, g_proj, g_up, g_down, kept_ref, given_ref)
    spread_rows = [tn(joins, table_sum[h].astype(BF16)) for h in range(HEADS)]
    ends = jnp.concatenate([p[:, 128:] for p in spread_rows] + [jnp.zeros((192, 32), F32)], axis=1)
    ends = ends + tn(gain_sums[...].astype(BF16), gain_lane)
    for e in range(64):
        at = slice(3 * e, 3 * e + 3)
        piece = jnp.concatenate([p[at, :128] for p in spread_rows] + [ends[at]], axis=0)
        strips_ref[e] = piece.astype(BF16)


def block_grads(last, core, blocks, rim, halves, landed, row_label, col_label):
    rows = 4 * WIN
    out = [
        ((4, WIN, D), BF16),
        ((WIN, D), BF16),
        ((64, 27, 128), BF16),
        ((64, 27, 128), BF16),
        ((64, 21, 128), BF16),
    ]
    scratch = [
        ((3 * D, D), BF16),
        ((D, D), BF16),
        ((FFN, D), BF16),
        ((D, FFN), BF16),
        ((3 * D, D), F32),
        ((D, D), F32),
        ((FFN, D), F32),
        ((D, FFN), F32),
        ((4, WIN, 2 * D), F32),
        ((HEADS, WIN, WIN), F32),
        ((HEADS * WIN, WIN), F32),
        ((HEADS * WIN, WIN), F32),
        ((HEADS * WIN, WIN), BF16),
        ((HEADS * WIN, WIN), BF16),
        ((HEADS * WIN, D), BF16),
        ((HEADS * WIN, D), BF16),
        ((HEADS, WIN, WIN), F32),
        ((rows, D), BF16),
        ((rows, D), BF16),
        ((rows, D), BF16),
        ((rows, FFN), BF16),
        ((rows, FFN), BF16),
        ((rows, D), BF16),
        ((3, rows, D), BF16),
        ((4, WIN, D), F32),
        ((8, D), F32),
    ]
    whole = pl.BlockSpec(memory_space=pltpu.VMEM)
    return pl.pallas_call(
        block_kernel,
        in_specs=[pl.BlockSpec(memory_space=pltpu.SMEM)] * 2 + [whole] * 9,
        out_specs=[whole] * len(out),
        out_shape=[jax.ShapeDtypeStruct(s, t) for s, t in out],
        scratch_shapes=[pltpu.VMEM(s, t) for s, t in scratch],
        compiler_params=pltpu.CompilerParams(vmem_limit_bytes=48 << 20),
        name="block_grads",
    )(last.reshape(1), core.reshape(1), *blocks, rim, halves, landed, row_label, col_label)


def one_hot(mask):
    return mask.astype(F32).astype(BF16)


def iota2(shape, axis):
    return lax.broadcasted_iota(jnp.int32, shape, axis)


def pack_kernel(
    spot_ref, types_ref, qkv_ref, proj_ref, up_ref, down_ref, gains_ref, table_ref, out_ref
):
    x_index, core, lat = spot_ref[0], spot_ref[1], spot_ref[2]

    first = up_ref[...].astype(F32)
    second = jnp.concatenate([qkv_ref[...].astype(F32), proj_ref[...].astype(F32)], axis=0)
    halves = []
    for rows in (first, second):
        rows = jnp.where(core == 0, rows[:6], rows[6:])
        halves.append(rows[:, :128])
        halves.append(jnp.concatenate([rows[:3, 128:], rows[3:, 128:]], axis=1))
    unit = iota2((1, 384), 1)
    unit = 12 * (unit // 6) + unit % 6 + 6 * core
    chosen = one_hot(iota2((FFN, 384), 0) == unit)
    downs = nn(down_ref[...], chosen)
    downs = [downs[:, 128 * t : 128 * (t + 1)] for t in range(3)]
    half = halves[:2] + downs + halves[2:]
    spots = one_hot(iota2((2, 128), 1) == 96 + iota2((2, 128), 0))
    gain_ends = tn(gains_ref[...], spots)
    wanted = jnp.full((8, 16), -1, jnp.int32)
    for a in range(4):
        wanted = jnp.where(iota2((8, 16), 0) == a, types_ref[a, lat], wanted)
    wanted = one_hot(iota2((8, 16), 1) == wanted)
    slabs = []
    for h in range(HEADS):
        slab = nn(wanted, table_ref[h])
        slab = jnp.concatenate([slab, jnp.zeros((8, 512 - 324), F32)], axis=1)
        slabs.append(pltpu.roll(slab, x_index * 36, 1))
    for a in range(4):
        slab = jnp.concatenate([p[a : a + 1] for p in slabs], axis=0)
        mains = [slab[:, WIN * r : WIN * r + 128] for r in range(3)]
        mains = [m[h : h + 1] for h in range(HEADS) for m in mains]
        ends = []
        for r in range(3):
            end = slab[:, WIN * r + 128 : WIN * (r + 1)]
            ends.append(jnp.concatenate([end[h : h + 1] for h in range(HEADS)], axis=1))
        ends = jnp.concatenate([jnp.concatenate(ends, axis=0), jnp.zeros((3, 32), F32)], axis=1)
        piece = jnp.concatenate(half + mains + [ends + gain_ends], axis=0).astype(BF16)
        for g in range(16):
            out_ref[4 * g + a] = piece


def finish_kernel(
    factor, types_ref, notes_ref, qkv_ref, proj_ref, up_ref, down_ref, gains_ref, table_ref
):
    notes = [notes_ref[i, :32, :].astype(F32) for i in range(4)]

    def six(note, at):
        ends = [note[at + 6 : at + 9, :64], note[at + 6 : at + 9, 64:]]
        return jnp.concatenate([note[at : at + 6], jnp.concatenate(ends, axis=0)], axis=1)

    sums = [(notes[c] + notes[2 + c]) * factor for c in range(2)]
    up_ref[:6, :] = six(sums[0], 0)
    up_ref[6:, :] = six(sums[1], 0)
    rest = six(sums[1], 18)
    qkv_ref[:6, :] = six(sums[0], 18)
    qkv_ref[6:, :] = rest[:3]
    proj_ref[...] = rest[3:]
    unit = iota2((1, 384), 1)
    unit = 12 * (unit // 6) + unit % 6
    downs = jnp.zeros((3, FFN), F32)
    for c in range(2):
        parts = []
        for note in (notes[c], notes[2 + c]):
            parts.append(
                jnp.concatenate([note[9 + 3 * t : 12 + 3 * t] for t in range(3)], axis=1)
            )
        parts = jnp.concatenate(parts, axis=0).astype(BF16)
        placed = nt(parts, one_hot(iota2((FFN, 384), 0) == unit + 6 * c))
        downs = downs + (placed[:3] + placed[3:])
    down_ref[...] = downs * factor
    gains = (notes[0] + notes[1] + notes[2] + notes[3])[27:28] * factor
    gains_ref[0:1, :] = gains[:, :3]
    gains_ref[1:2, :] = gains[:, 3:6]
    wanted = jnp.zeros((16, 16), jnp.int32)
    for i in range(4):
        for a in range(4):
            wanted = jnp.where(iota2((16, 16), 1) == 4 * i + a, types_ref[a, i], wanted)
    wanted = one_hot(iota2((16, 16), 0) == wanted)
    tables = [notes_ref[i, 32:104, :].astype(F32) for i in range(4)]
    for h in range(HEADS):
        lanes = []
        for j in range(3):
            at = 4 * (3 * h + j)
            terms = jnp.concatenate([t[at : at + 4] for t in tables], axis=0).astype(BF16)
            lanes.append(nn(wanted, terms))
        table_ref[h] = jnp.concatenate(lanes, axis=1)[:, :324]


def small_call(kernel, args, scalars, out, scratch, name):
    whole = pl.BlockSpec(memory_space=pltpu.VMEM)
    flat = pl.BlockSpec(memory_space=pltpu.SMEM)
    return pl.pallas_call(
        kernel,
        in_specs=[flat] * scalars + [whole] * (len(args) - scalars),
        out_specs=[whole] * len(out),
        out_shape=[jax.ShapeDtypeStruct(s, t) for s, t in out],
        scratch_shapes=[pltpu.VMEM(s, t) for s, t in scratch],
        name=name,
    )(*args)


def shards(
    inputs,
    cotangent,
    qkv_weight,
    proj_weight,
    up_weight,
    down_weight,
    norm_gains,
    bias_table,
    type_of,
    region,
):
    lat_index = lax.axis_index(LAT)
    core = lax.axis_index("core")
    x_index = lax.axis_index("x")
    type_count = bias_table.shape[0]
    positions = type_of.shape[0]
    own = bias_table.shape[2]
    groups = lax.axis_size("yl") * lax.axis_size("z")
    members = lax.axis_size("x")
    lons = groups * members

    def side_by_side(one, two):
        both = jnp.roll(jnp.concatenate([one, two], axis=-1), -1, axis=0)
        return both.reshape(positions, WIN // 2, 2 * D)

    rows = WLAT // 2
    arrived = [passed_along(a[:, :rows], LAT, -1) for a in (inputs, cotangent)]
    spot = jnp.stack([x_index, core, lat_index]).astype(jnp.int32)
    weights = [w.T for w in (qkv_weight, proj_weight, up_weight, down_weight)]
    weights += [norm_gains, bias_table.transpose(1, 0, 2)]
    (parcel,) = small_call(
        pack_kernel, (spot, type_of, *weights), 2, [((lons, 48, 128), BF16)], [], "pack"
    )

    parcel, arrived = lax.optimization_barrier((parcel, arrived))
    cells = side_by_side(inputs[:, rows:], cotangent[:, rows:])
    cells = jnp.concatenate([cells, side_by_side(*arrived)], axis=1)
    cells = jnp.concatenate([cells, cells[: members - 1]], axis=0)
    cells = lax.dynamic_slice_in_dim(cells, x_index, members, 0)
    blocks = [cells[0]] + [passed_along(cells[k], ("x",), k) for k in range(1, members)]
    landed = lax.all_to_all(parcel, LON, 0, 0)
    is_first = [x_index == k for k in range(members)]
    rim = blocks[0]
    for k in range(1, members):
        rim = jnp.where(is_first[k], blocks[k], rim)
    rim = passed_along(rim, ("yl", "z"), -1)
    landed, rim = lax.optimization_barrier((landed, rim))
    last = (x_index + 1) % members
    halves = passed_along(landed, ("core",), 1)

    labels = lax.dynamic_slice(region, (x_index * WPL, jnp.int32(0)), (WPL, WLAT))
    labels = jnp.broadcast_to(labels[:, :, None], (WPL, WLAT, WLON)).reshape(WIN)
    back, rim, kept, given, strips = block_grads(
        last, core, blocks, rim, halves, landed, labels.reshape(WIN, 1), labels.reshape(1, WIN)
    )

    g_half = kept.astype(F32) + passed_along(given, ("core",), 1).astype(F32)
    parcel = jnp.concatenate([g_half.astype(BF16), strips], axis=1)
    parcel, rim = lax.optimization_barrier((parcel, rim))
    rim = passed_along(rim, ("yl", "z"), 1)
    returned = lax.all_to_all(parcel, LON, 0, 0)
    blocks = [jnp.where(is_first[k], back[k] + rim, back[k]) for k in range(members)]
    blocks = [blocks[0]] + [passed_along(blocks[k], ("x",), -k) for k in range(1, members)]
    back = jnp.stack(blocks + blocks[: members - 1])
    back = lax.dynamic_slice_in_dim(back, (members - x_index) % members, members, 0)
    back = back.reshape(positions, 2, WIN // 2, D)
    arrived = passed_along(back[:, 1], LAT, 1)
    back = jnp.stack([arrived, back[:, 0]], axis=1)
    back = back.reshape(positions, 2, WPL, WLAT // 2, WLON, D).transpose(0, 2, 1, 3, 4, 5)
    grad_input = jnp.roll(back.reshape(inputs.shape), 1, axis=0)

    returned = returned.astype(F32)
    half_sum = jnp.sum(returned[:, :27], axis=0)
    strip_sum = jnp.sum(returned[:, 27:].reshape(groups, members, 21, 128), axis=0)
    ends = strip_sum[:, 18:, :96].reshape(positions, 3, HEADS, 16).transpose(0, 2, 1, 3)
    table_part = jnp.concatenate(
        [strip_sum[:, :18].reshape(positions, HEADS, 3, 128), ends], axis=3
    ).reshape(positions, HEADS, 3 * WIN)
    table_part = lax.dynamic_slice_in_dim(table_part, x_index * 36, own, 2)
    gain_sum = jnp.sum(strip_sum[:, 18:, 96:98], axis=0).T.reshape(-1)
    note = jnp.pad(table_part, ((0, 0), (0, 0), (0, 384 - own))).reshape(positions, 18, 128)
    note = note.transpose(1, 0, 2).reshape(72, 128)
    gain_row = jnp.pad(gain_sum.reshape(1, 6), ((0, 4), (0, 122)))
    note = jnp.concatenate([half_sum, gain_row, note], axis=0).astype(BF16)
    notes = lax.all_gather(note, LAT, axis=0)
    factor = 1.0 / math.sqrt(inputs.shape[0] * inputs.shape[1] * inputs.shape[2] * 4 * lons)
    shapes = [w.shape[::-1] for w in (qkv_weight, proj_weight, up_weight, down_weight)]
    shapes += [norm_gains.shape, (HEADS, type_count, own)]
    out = [(shape, F32) for shape in shapes]
    kernel = functools.partial(finish_kernel, factor)
    grads = small_call(kernel, (type_of, notes), 1, out, [], "finish")
    table = grads[5].transpose(1, 0, 2)
    return (grad_input, grads[0].T, grads[1].T, grads[2].T, grads[3].T, grads[4], table)


def solution(mesh):
    finer = Mesh(mesh.devices.reshape(2, 2, 2, 8, 4), ("yh", "core", "yl", "z", "x"))
    return jax.shard_map(
        shards,
        mesh=finer,
        in_specs=(
            P(None, LAT, LON, None),
            P(None, LAT, LON, None),
            P(None, LON),
            P(None, LON),
            P(None, LON),
            P(None, LON),
            P(None, LON),
            P(None, None, LON),
            P(),
            P(None, LAT),
        ),
        out_specs=(
            P(None, LAT, LON, None),
            P(None, LON),
            P(None, LON),
            P(None, LON),
            P(None, LON),
            P(None, LON),
            P(None, None, LON),
        ),
        check_vma=False,
    )
```

```python
import functools
import math

import jax
import jax.numpy as jnp
from jax import lax
from jax.experimental import pallas as pl
from jax.experimental.pallas import tpu as pltpu
from jax.sharding import Mesh, PartitionSpec as P

WPL = 2
WLAT = 6
WLON = 12
WIN = 144
D = 192
HEADS = 6
HEAD = 32
FFN = 768
LON = ("yl", "z", "x")
LAT = ("yh", "core")
F32 = jnp.float32
BF16 = jnp.bfloat16


def passed_along(block, axes, distance):
    size = math.prod(lax.axis_size(a) for a in axes)
    return lax.ppermute(block, axes, [((i - distance) % size, i) for i in range(size)])


def layer_norm(values):
    row_mean = jnp.mean(values, axis=-1, keepdims=True)
    centred = values - row_mean
    variance = jnp.mean(centred * centred, axis=-1, keepdims=True)
    inv_std = lax.rsqrt(variance + 1e-05)
    return (centred * inv_std, inv_std)


def norm_back(d_normed, normed, inv_std):
    return inv_std * (
        d_normed
        - jnp.mean(d_normed, axis=-1, keepdims=True)
        - normed * jnp.mean(d_normed * normed, axis=-1, keepdims=True)
    )


def gelu_pair(pre_act):
    cumul = 0.5 * (1.0 + lax.erf(pre_act * 0.7071067811865476))
    density = jnp.exp(-0.5 * pre_act * pre_act) * 0.3989422804014327
    return (pre_act * cumul, cumul + pre_act * density)


def spread(a, b, contract):
    return lax.dot_general(a, b, ((contract[0], contract[1]), ((), ())), preferred_element_type=F32)


def nt(a, b):
    return spread(a, b, ((1,), (1,)))


def nn(a, b):
    return spread(a, b, ((1,), (0,)))


def tn(a, b):
    return spread(a, b, ((0,), (0,)))


def swap_quarters(rows):
    return jnp.concatenate([rows[:36], rows[72:108], rows[36:72], rows[108:]], axis=0)


def unpack_weights(core, mine_ref, other_ref, qkv_ref, proj_ref, up_ref, down_ref):
    def stack(pieces):
        return jnp.concatenate(pieces, axis=0).astype(BF16)

    for g in range(4):
        mine = [mine_ref[16 * g + i, :32, :].astype(F32)[:27] for i in range(16)]
        other = [other_ref[16 * g + i, :32, :].astype(F32)[:27] for i in range(16)]
        v = [
            [jnp.where(core == c, a, b) for a, b in zip(mine, other)] for c in range(2)
        ]
        for c in range(2):
            rows = slice(c * 384 + 96 * g, c * 384 + 96 * (g + 1))
            up_ref[rows, :128] = stack([p[:6] for p in v[c]])
            up_ref[rows, 128:] = stack([p[6:9, s : s + 64] for p in v[c] for s in (0, 64)])
            for t in range(3):
                cols = slice(c * 384 + 128 * t, c * 384 + 128 * (t + 1))
                down_ref[48 * g : 48 * (g + 1), cols] = stack(
                    [p[9 + 3 * t : 12 + 3 * t] for p in v[c]]
                )
        rows = slice(144 * g, 144 * (g + 1))
        pairs = list(zip(v[0], v[1]))
        qkv_ref[rows, :128] = stack([q for a, b in pairs for q in (a[18:24], b[18:21])])
        qkv_ref[rows, 128:] = stack(
            [q for a, b in pairs for q in (a[24:27, :64], a[24:27, 64:], b[24:27, :64])]
        )
        rows = slice(48 * g, 48 * (g + 1))
        proj_ref[rows, :128] = stack([b[21:24] for b in v[1]])
        proj_ref[rows, 128:] = stack([b[24:27, 64:] for b in v[1]])


def pack_grads(core, g_qkv, g_proj, g_up, g_down, kept_ref, given_ref):
    def tails(ref, at, gap):
        return [ref[at : at + 3, 128:], ref[at + gap : at + gap + 3, 128:]]

    for e in range(64):
        pieces = []
        for c in range(2):
            at = c * 384 + 6 * e
            ups = [g_up[at : at + 6, :128], jnp.concatenate(tails(g_up, at, 3), axis=1)]
            downs = [
                g_down[3 * e : 3 * e + 3, c * 384 + 128 * t : c * 384 + 128 * (t + 1)]
                for t in range(3)
            ]
            if c == 0:
                rest = [g_qkv[9 * e : 9 * e + 6, :128]]
                ends = tails(g_qkv, 9 * e, 3)
            else:
                rest = [g_qkv[9 * e + 6 : 9 * e + 9, :128], g_proj[3 * e : 3 * e + 3, :128]]
                ends = [g_qkv[9 * e + 6 : 9 * e + 9, 128:], g_proj[3 * e : 3 * e + 3, 128:]]
            rest.append(jnp.concatenate(ends, axis=1))
            pieces.append(jnp.concatenate(ups + downs + rest, axis=0))
        kept_ref[e] = jnp.where(core == 0, pieces[0], pieces[1]).astype(BF16)
        given_ref[e] = jnp.where(core == 0, pieces[1], pieces[0]).astype(BF16)


def block_kernel(
    last_ref,
    core_ref,
    b0,
    b1,
    b2,
    b3,
    rim_ref,
    halves_ref,
    landed_ref,
    row_label_ref,
    col_label_ref,
    back_ref,
    back_rim_ref,
    kept_ref,
    given_ref,
    strips_ref,
    qkv_ref,
    proj_ref,
    up_ref,
    down_ref,
    g_qkv,
    g_proj,
    g_up,
    g_down,
    tokens,
    bias_full,
    probs,
    d_probs,
    probs_b,
    scores_b,
    heads_q,
    heads_d,
    table_sum,
    s_one,
    s_two,
    att_all,
    hid_all,
    dhid_all,
    dmid_all,
    dpack_all,
    d_tokens,
    gain_sums,
):
    factor = 1.0 / math.sqrt(HEAD)
    last = last_ref[0]
    blocks = (b0, b1, b2, b3)
    place = lax.broadcasted_iota(jnp.int32, (WIN, 1), 0) % WLON
    is_left = place < WLON // 2
    same = row_label_ref[...] == col_label_ref[...]
    unpack_weights(core_ref[0], landed_ref, halves_ref, qkv_ref, proj_ref, up_ref, down_ref)
    source = lax.broadcasted_iota(jnp.int32, (WIN, 192), 1)
    target = lax.broadcasted_iota(jnp.int32, (WIN, 192), 0)
    held = 9 * (source // 12) + 2 * (source // 3 % 4) + source % 3
    joins = (held == target).astype(F32).astype(BF16)
    strips = [landed_ref[e, 24:48, :].astype(F32)[3:] for e in range(64)]
    ends = jnp.concatenate([p[18:] for p in strips], axis=0).astype(BF16)
    bias_ends = nn(joins, ends)
    for h in range(HEADS):
        main = jnp.concatenate([p[3 * h : 3 * h + 3] for p in strips], axis=0).astype(BF16)
        row = jnp.concatenate([nn(joins, main), bias_ends[:, 16 * h : 16 * h + 16]], axis=1)
        bias_full[h] = jnp.where(same, row, -jnp.inf)
        table_sum[h] = jnp.zeros((WIN, WIN), F32)
    gain_lane = lax.broadcasted_iota(jnp.int32, (8, 128), 1) - 96
    gain_lane = gain_lane == lax.broadcasted_iota(jnp.int32, (8, 128), 0)
    gain_lane = gain_lane.astype(F32).astype(BF16)
    gains = nt(gain_lane, ends)
    gain_sums[...] = jnp.zeros_like(gain_sums)
    rim = swap_quarters(rim_ref[...].astype(F32))
    natural = [swap_quarters(b[...].astype(F32)) for b in blocks]
    for k in range(4):
        ahead = jnp.where(last == k, rim, natural[k - 1])
        fore = jnp.concatenate([natural[k][6:], natural[k][:6]], axis=0)
        rear = jnp.concatenate([ahead[-6:], ahead[:-6]], axis=0)
        tokens[k] = jnp.where(is_left, fore, rear)
    gain_one = gains[0:1, :]
    gain_two = gains[1:2, :]
    lane = lax.broadcasted_iota(jnp.int32, (1, D), 1) // HEAD
    masks = [(lane == h).astype(BF16) for h in range(HEADS)]
    of_head = [slice(h * WIN, (h + 1) * WIN) for h in range(HEADS)]

    def own_lanes(stacked):
        out = stacked[of_head[0]]
        for h in range(1, HEADS):
            out = jnp.where(lane == h, stacked[of_head[h]], out)
        return out

    def one_window(w, carry):
        at = pl.multiple_of(w * WIN, 16)
        rows = pl.ds(at, WIN)
        both = tokens[w]
        cells = both[:, :D]
        cot = both[:, D:]
        cot_b = cot.astype(BF16)
        normed_one, inv_one = layer_norm(cells)
        scaled_one = (normed_one * gain_one).astype(BF16)
        s_one[rows, :] = scaled_one
        queries = nt(scaled_one, qkv_ref[0:D, :]).astype(BF16)
        key_rows = nt(scaled_one, qkv_ref[D : 2 * D, :]).astype(BF16)
        values = nt(scaled_one, qkv_ref[2 * D :, :]).astype(BF16)
        for h in range(HEADS):
            heads_q[of_head[h], :] = queries * masks[h]
        probs[...] = nt(heads_q[...], key_rows)
        for h in range(HEADS):
            scores = probs[of_head[h], :] * factor + bias_full[h]
            raised = jnp.exp(scores - jnp.max(scores, axis=-1, keepdims=True))
            p = raised * (1.0 / jnp.sum(raised, axis=-1, keepdims=True))
            probs[of_head[h], :] = p
            probs_b[of_head[h], :] = p.astype(BF16)
        attended = own_lanes(nn(probs_b[...], values))
        attended = attended.astype(BF16)
        att_all[rows, :] = attended
        middle = cells + nt(attended, proj_ref[...])
        normed_two, inv_two = layer_norm(middle)
        scaled_two = (normed_two * gain_two).astype(BF16)
        s_two[rows, :] = scaled_two
        d_htwo = jnp.zeros((WIN, D), F32)
        for c in range(3):
            part = slice(c * 256, (c + 1) * 256)
            pre_act = nt(scaled_two, up_ref[part, :])
            activated, slope = gelu_pair(pre_act)
            hid_all[rows, part] = activated.astype(BF16)
            d_hidden = (nn(cot_b, down_ref[:, part]) * slope).astype(BF16)
            dhid_all[rows, part] = d_hidden
            d_htwo = d_htwo + nn(d_hidden, up_ref[part, :])
        gain_sums[1:2, :] += jnp.sum(d_htwo * normed_two, axis=0, keepdims=True)
        d_middle = cot + norm_back(d_htwo * gain_two, normed_two, inv_two)
        d_middle_b = d_middle.astype(BF16)
        dmid_all[rows, :] = d_middle_b
        d_att = nn(d_middle_b, proj_ref[...]).astype(BF16)
        for h in range(HEADS):
            heads_d[of_head[h], :] = d_att * masks[h]
        d_probs[...] = nt(heads_d[...], values)
        for h in range(HEADS):
            p = probs[of_head[h], :]
            d_prob = d_probs[of_head[h], :]
            d_score = p * (d_prob - jnp.sum(p * d_prob, axis=-1, keepdims=True))
            table_sum[h] += d_score
            scores_b[of_head[h], :] = d_score.astype(BF16)
        d_queries = own_lanes(nn(scores_b[...], key_rows))
        d_keys = tn(scores_b[...], heads_q[...])
        d_values = tn(probs_b[...], heads_d[...])
        d_q = (d_queries * factor).astype(BF16)
        d_k = (d_keys * factor).astype(BF16)
        d_v = d_values.astype(BF16)
        dpack_all[0, rows, :] = d_q
        dpack_all[1, rows, :] = d_k
        dpack_all[2, rows, :] = d_v
        d_hone = (
            nn(d_q, qkv_ref[0:D, :]) + nn(d_k, qkv_ref[D : 2 * D, :]) + nn(d_v, qkv_ref[2 * D :, :])
        )
        gain_sums[0:1, :] += jnp.sum(d_hone * normed_one, axis=0, keepdims=True)
        d_tokens[w] = d_middle + norm_back(d_hone * gain_one, normed_one, inv_one)
        return carry

    lax.fori_loop(0, 4, one_window, 0, unroll=4)
    for k in range(4):
        mine, following = d_tokens[k], d_tokens[(k + 1) % 4]
        fore = jnp.concatenate([mine[-6:], mine[:-6]], axis=0)
        rear = jnp.concatenate([following[6:], following[:6]], axis=0)
        first = (k + 1) % 4 == last
        back_ref[k] = swap_quarters(
            jnp.where(is_left, jnp.where(first, 0.0, rear), fore)
        ).astype(BF16)

        @pl.when(first)
        def _():
            back_rim_ref[...] = swap_quarters(jnp.where(is_left, rear, 0.0)).astype(BF16)

    for part in range(3):
        g_qkv[part * D : (part + 1) * D, :] = tn(dpack_all[part], s_one[...])
    g_proj[...] = tn(dmid_all[...], att_all[...])
    cots = jnp.concatenate([tokens[k][:, D:] for k in range(4)], axis=0).astype(BF16)
    g_down[...] = tn(cots, hid_all[...])
    g_up[...] = tn(dhid_all[...], s_two[...])
    pack_grads(core_ref[0], g_qkv, g_proj, g_up, g_down, kept_ref, given_ref)
    spread_rows = [tn(joins, table_sum[h].astype(BF16)) for h in range(HEADS)]
    ends = jnp.concatenate([p[:, 128:] for p in spread_rows] + [jnp.zeros((192, 32), F32)], axis=1)
    ends = ends + tn(gain_sums[...].astype(BF16), gain_lane)
    for e in range(64):
        at = slice(3 * e, 3 * e + 3)
        piece = jnp.concatenate([p[at, :128] for p in spread_rows] + [ends[at]], axis=0)
        strips_ref[e] = piece.astype(BF16)


def block_grads(last, core, blocks, rim, halves, landed, row_label, col_label):
    rows = 4 * WIN
    out = [
        ((4, WIN, D), BF16),
        ((WIN, D), BF16),
        ((64, 27, 128), BF16),
        ((64, 27, 128), BF16),
        ((64, 21, 128), BF16),
    ]
    scratch = [
        ((3 * D, D), BF16),
        ((D, D), BF16),
        ((FFN, D), BF16),
        ((D, FFN), BF16),
        ((3 * D, D), F32),
        ((D, D), F32),
        ((FFN, D), F32),
        ((D, FFN), F32),
        ((4, WIN, 2 * D), F32),
        ((HEADS, WIN, WIN), F32),
        ((HEADS * WIN, WIN), F32),
        ((HEADS * WIN, WIN), F32),
        ((HEADS * WIN, WIN), BF16),
        ((HEADS * WIN, WIN), BF16),
        ((HEADS * WIN, D), BF16),
        ((HEADS * WIN, D), BF16),
        ((HEADS, WIN, WIN), F32),
        ((rows, D), BF16),
        ((rows, D), BF16),
        ((rows, D), BF16),
        ((rows, FFN), BF16),
        ((rows, FFN), BF16),
        ((rows, D), BF16),
        ((3, rows, D), BF16),
        ((4, WIN, D), F32),
        ((8, D), F32),
    ]
    whole = pl.BlockSpec(memory_space=pltpu.VMEM)
    return pl.pallas_call(
        block_kernel,
        in_specs=[pl.BlockSpec(memory_space=pltpu.SMEM)] * 2 + [whole] * 9,
        out_specs=[whole] * len(out),
        out_shape=[jax.ShapeDtypeStruct(s, t) for s, t in out],
        scratch_shapes=[pltpu.VMEM(s, t) for s, t in scratch],
        compiler_params=pltpu.CompilerParams(vmem_limit_bytes=48 << 20),
        name="block_grads",
    )(last.reshape(1), core.reshape(1), *blocks, rim, halves, landed, row_label, col_label)


def one_hot(mask):
    return mask.astype(F32).astype(BF16)


def iota2(shape, axis):
    return lax.broadcasted_iota(jnp.int32, shape, axis)


def pack_kernel(
    types_ref, qkv_ref, proj_ref, up_ref, down_ref, gains_ref, table_ref, out_ref
):
    x_index, core, lat = lax.axis_index("x"), lax.axis_index("core"), lax.axis_index(LAT)

    first = up_ref[...].astype(F32)
    second = jnp.concatenate([qkv_ref[...].astype(F32), proj_ref[...].astype(F32)], axis=0)
    halves = []
    for rows in (first, second):
        rows = jnp.where(core == 0, rows[:6], rows[6:])
        halves.append(rows[:, :128])
        halves.append(jnp.concatenate([rows[:3, 128:], rows[3:, 128:]], axis=1))
    unit = iota2((1, 384), 1)
    unit = 12 * (unit // 6) + unit % 6 + 6 * core
    chosen = one_hot(iota2((FFN, 384), 0) == unit)
    downs = nn(down_ref[...], chosen)
    downs = [downs[:, 128 * t : 128 * (t + 1)] for t in range(3)]
    half = halves[:2] + downs + halves[2:]
    spots = one_hot(iota2((2, 128), 1) == 96 + iota2((2, 128), 0))
    gain_ends = tn(gains_ref[...], spots)
    wanted = jnp.full((8, 16), -1, jnp.int32)
    for a in range(4):
        wanted = jnp.where(iota2((8, 16), 0) == a, types_ref[a, lat], wanted)
    wanted = one_hot(iota2((8, 16), 1) == wanted)
    slabs = []
    for h in range(HEADS):
        slab = nn(wanted, table_ref[h])
        slab = jnp.concatenate([slab, jnp.zeros((8, 512 - 324), F32)], axis=1)
        slabs.append(pltpu.roll(slab, x_index * 36, 1))
    for a in range(4):
        slab = jnp.concatenate([p[a : a + 1] for p in slabs], axis=0)
        mains = [slab[:, WIN * r : WIN * r + 128] for r in range(3)]
        mains = [m[h : h + 1] for h in range(HEADS) for m in mains]
        ends = []
        for r in range(3):
            end = slab[:, WIN * r + 128 : WIN * (r + 1)]
            ends.append(jnp.concatenate([end[h : h + 1] for h in range(HEADS)], axis=1))
        ends = jnp.concatenate([jnp.concatenate(ends, axis=0), jnp.zeros((3, 32), F32)], axis=1)
        piece = jnp.concatenate(half + mains + [ends + gain_ends], axis=0).astype(BF16)
        for g in range(16):
            out_ref[4 * g + a] = piece


def finish_kernel(
    factor, types_ref, notes_ref, qkv_ref, proj_ref, up_ref, down_ref, gains_ref, table_ref
):
    notes = [notes_ref[i, :32, :].astype(F32) for i in range(4)]

    def six(note, at):
        ends = [note[at + 6 : at + 9, :64], note[at + 6 : at + 9, 64:]]
        return jnp.concatenate([note[at : at + 6], jnp.concatenate(ends, axis=0)], axis=1)

    sums = [(notes[c] + notes[2 + c]) * factor for c in range(2)]
    up_ref[:6, :] = six(sums[0], 0)
    up_ref[6:, :] = six(sums[1], 0)
    rest = six(sums[1], 18)
    qkv_ref[:6, :] = six(sums[0], 18)
    qkv_ref[6:, :] = rest[:3]
    proj_ref[...] = rest[3:]
    unit = iota2((1, 384), 1)
    unit = 12 * (unit // 6) + unit % 6
    downs = jnp.zeros((3, FFN), F32)
    for c in range(2):
        parts = []
        for note in (notes[c], notes[2 + c]):
            parts.append(
                jnp.concatenate([note[9 + 3 * t : 12 + 3 * t] for t in range(3)], axis=1)
            )
        parts = jnp.concatenate(parts, axis=0).astype(BF16)
        placed = nt(parts, one_hot(iota2((FFN, 384), 0) == unit + 6 * c))
        downs = downs + (placed[:3] + placed[3:])
    down_ref[...] = downs * factor
    gains = (notes[0] + notes[1] + notes[2] + notes[3])[27:28] * factor
    gains_ref[0:1, :] = gains[:, :3]
    gains_ref[1:2, :] = gains[:, 3:6]
    wanted = jnp.zeros((16, 16), jnp.int32)
    for i in range(4):
        for a in range(4):
            wanted = jnp.where(iota2((16, 16), 1) == 4 * i + a, types_ref[a, i], wanted)
    wanted = one_hot(iota2((16, 16), 0) == wanted)
    tables = [notes_ref[i, 32:104, :].astype(F32) for i in range(4)]
    for h in range(HEADS):
        lanes = []
        for j in range(3):
            at = 4 * (3 * h + j)
            terms = jnp.concatenate([t[at : at + 4] for t in tables], axis=0).astype(BF16)
            lanes.append(nn(wanted, terms))
        table_ref[h] = jnp.concatenate(lanes, axis=1)[:, :324]


def small_call(kernel, args, scalars, out, scratch, name):
    whole = pl.BlockSpec(memory_space=pltpu.VMEM)
    flat = pl.BlockSpec(memory_space=pltpu.SMEM)
    return pl.pallas_call(
        kernel,
        in_specs=[flat] * scalars + [whole] * (len(args) - scalars),
        out_specs=[whole] * len(out),
        out_shape=[jax.ShapeDtypeStruct(s, t) for s, t in out],
        scratch_shapes=[pltpu.VMEM(s, t) for s, t in scratch],
        name=name,
    )(*args)


def shards(
    inputs,
    cotangent,
    qkv_weight,
    proj_weight,
    up_weight,
    down_weight,
    norm_gains,
    bias_table,
    type_of,
    region,
):
    lat_index = lax.axis_index(LAT)
    core = lax.axis_index("core")
    x_index = lax.axis_index("x")
    type_count = bias_table.shape[0]
    positions = type_of.shape[0]
    own = bias_table.shape[2]
    groups = lax.axis_size("yl") * lax.axis_size("z")
    members = lax.axis_size("x")
    lons = groups * members

    def side_by_side(one, two):
        both = jnp.roll(jnp.concatenate([one, two], axis=-1), -1, axis=0)
        return both.reshape(positions, WIN // 2, 2 * D)

    rows = WLAT // 2
    arrived = [passed_along(a[:, :rows], LAT, -1) for a in (inputs, cotangent)]
    weights = [w.T for w in (qkv_weight, proj_weight, up_weight, down_weight)]
    weights += [norm_gains, bias_table.transpose(1, 0, 2)]
    (parcel,) = small_call(
        pack_kernel, (type_of, *weights), 1, [((lons, 48, 128), BF16)], [], "pack"
    )

    parcel, arrived = lax.optimization_barrier((parcel, arrived))
    cells = side_by_side(inputs[:, rows:], cotangent[:, rows:])
    cells = jnp.concatenate([cells, side_by_side(*arrived)], axis=1)
    cells = jnp.concatenate([cells, cells[: members - 1]], axis=0)
    cells = lax.dynamic_slice_in_dim(cells, x_index, members, 0)
    blocks = [cells[0]] + [passed_along(cells[k], ("x",), k) for k in range(1, members)]
    landed = lax.all_to_all(parcel, LON, 0, 0)
    is_first = [x_index == k for k in range(members)]
    rim = blocks[0]
    for k in range(1, members):
        rim = jnp.where(is_first[k], blocks[k], rim)
    rim = passed_along(rim, ("yl", "z"), -1)
    landed, rim = lax.optimization_barrier((landed, rim))
    last = (x_index + 1) % members
    halves = passed_along(landed, ("core",), 1)

    labels = lax.dynamic_slice(region, (x_index * WPL, jnp.int32(0)), (WPL, WLAT))
    labels = jnp.broadcast_to(labels[:, :, None], (WPL, WLAT, WLON)).reshape(WIN)
    back, rim, kept, given, strips = block_grads(
        last, core, blocks, rim, halves, landed, labels.reshape(WIN, 1), labels.reshape(1, WIN)
    )

    g_half = kept.astype(F32) + passed_along(given, ("core",), 1).astype(F32)
    parcel = jnp.concatenate([g_half.astype(BF16), strips], axis=1)
    parcel, rim = lax.optimization_barrier((parcel, rim))
    rim = passed_along(rim, ("yl", "z"), 1)
    returned = lax.all_to_all(parcel, LON, 0, 0)
    blocks = [jnp.where(is_first[k], back[k] + rim, back[k]) for k in range(members)]
    blocks = [blocks[0]] + [passed_along(blocks[k], ("x",), -k) for k in range(1, members)]
    back = jnp.stack(blocks + blocks[: members - 1])
    back = lax.dynamic_slice_in_dim(back, (members - x_index) % members, members, 0)
    back = back.reshape(positions, 2, WIN // 2, D)
    arrived = passed_along(back[:, 1], LAT, 1)
    back = jnp.stack([arrived, back[:, 0]], axis=1)
    back = back.reshape(positions, 2, WPL, WLAT // 2, WLON, D).transpose(0, 2, 1, 3, 4, 5)
    grad_input = jnp.roll(back.reshape(inputs.shape), 1, axis=0)

    returned = returned.astype(F32)
    half_sum = jnp.sum(returned[:, :27], axis=0)
    strip_sum = jnp.sum(returned[:, 27:].reshape(groups, members, 21, 128), axis=0)
    ends = strip_sum[:, 18:, :96].reshape(positions, 3, HEADS, 16).transpose(0, 2, 1, 3)
    table_part = jnp.concatenate(
        [strip_sum[:, :18].reshape(positions, HEADS, 3, 128), ends], axis=3
    ).reshape(positions, HEADS, 3 * WIN)
    table_part = lax.dynamic_slice_in_dim(table_part, x_index * 36, own, 2)
    gain_sum = jnp.sum(strip_sum[:, 18:, 96:98], axis=0).T.reshape(-1)
    note = jnp.pad(table_part, ((0, 0), (0, 0), (0, 384 - own))).reshape(positions, 18, 128)
    note = note.transpose(1, 0, 2).reshape(72, 128)
    gain_row = jnp.pad(gain_sum.reshape(1, 6), ((0, 4), (0, 122)))
    note = jnp.concatenate([half_sum, gain_row, note], axis=0).astype(BF16)
    notes = lax.all_gather(note, LAT, axis=0)
    factor = 1.0 / math.sqrt(inputs.shape[0] * inputs.shape[1] * inputs.shape[2] * 4 * lons)
    shapes = [w.shape[::-1] for w in (qkv_weight, proj_weight, up_weight, down_weight)]
    shapes += [norm_gains.shape, (HEADS, type_count, own)]
    out = [(shape, F32) for shape in shapes]
    kernel = functools.partial(finish_kernel, factor)
    grads = small_call(kernel, (type_of, notes), 1, out, [], "finish")
    table = grads[5].transpose(1, 0, 2)
    return (grad_input, grads[0].T, grads[1].T, grads[2].T, grads[3].T, grads[4], table)


def solution(mesh):
    finer = Mesh(mesh.devices.reshape(2, 2, 2, 8, 4), ("yh", "core", "yl", "z", "x"))
    return jax.shard_map(
        shards,
        mesh=finer,
        in_specs=(
            P(None, LAT, LON, None),
            P(None, LAT, LON, None),
            P(None, LON),
            P(None, LON),
            P(None, LON),
            P(None, LON),
            P(None, LON),
            P(None, None, LON),
            P(),
            P(None, LAT),
        ),
        out_specs=(
            P(None, LAT, LON, None),
            P(None, LON),
            P(None, LON),
            P(None, LON),
            P(None, LON),
            P(None, LON),
            P(None, None, LON),
        ),
        check_vma=False,
    )
```
